512 devices in a mesh: bead: 16 (over x, z_hi), space: 32 (over z_lo, y, core).
Axes of the slice: x: 4, y: 4, z: 16 (z_hi: 4, z_lo: 4; z = z_hi * 4 + z_lo), core: 2. Of those that a mesh axis runs over, the one named last changes fastest.
Arguments:
- positions: float32 [32, 3, 512, 128], P('bead', None, 'space'), may hold values from -0.1 to 1.1
- momenta: float32 [32, 3, 512, 128], P('bead', None, 'space'), may hold values from -6 to 6
- molecules: int32 [512, 42, 3], P('space'), may hold values from 0 to 128, as said below
Outputs:
- final_positions: float32 [32, 3, 512, 128], P('bead', None, 'space')
- final_momenta: float32 [32, 3, 512, 128], P('bead', None, 'space')
The draws below stay inside these ranges and needn't reach their ends.
Inputs may be any that keep to these rules, and one draw needn't show every extreme that they name: In each cell, the slots of all listed atoms differ; used molecules come first and unused ones carry 128 in all three places; each cell has 21 to 42 used molecules.
All inputs are finite; a program needn't handle non-finite values.
Results may differ from the reference program's by a relative error of at most 0.0003.
Values sent between devices are 32-bit elements; how exact they have to be, the bound alone decides.
A program may use at most 64 MiB of HBM per device.

```python
import jax
import jax.numpy as jnp
from jax import lax

BEADS = 32
SLOTS = 128
MOLS = 42
REACH = 1
NEIGH = 3
CELLS = 512


def molecule_table(key):
    base_key = jax.random.fold_in(key, 17)
    count_key, full_key, order_key = jax.random.split(base_key, 3)
    counts = jax.random.randint(count_key, (CELLS,), MOLS // 2, MOLS + 1)
    full_cell = jax.random.randint(full_key, (), 0, CELLS)
    counts = jnp.where(jnp.arange(CELLS) == full_cell, MOLS, counts)
    slot_rows = jnp.broadcast_to(jnp.arange(SLOTS, dtype=jnp.int32), (CELLS, SLOTS))
    shuffled = jax.random.permutation(order_key, slot_rows, axis=1, independent=True)
    chosen = shuffled[:, :3 * MOLS].reshape(CELLS, MOLS, 3)
    used = jnp.arange(MOLS)[None, :, None] < counts[:, None, None]
    return jnp.where(used, chosen, SLOTS).astype(jnp.int32)


def draw_molecules(key, part):
    return molecule_table(key)


def draw_momenta(key, part):
    moment_key = jax.random.fold_in(key, 73)
    sign_key, size_key = jax.random.split(moment_key, 2)
    shape = (BEADS, 3, CELLS, SLOTS)
    flips = jax.random.bernoulli(sign_key, 0.5, shape)
    signs = jnp.where(flips, 1.0, -1.0).astype(jnp.float32)
    magnitude = jax.random.uniform(size_key, shape, jnp.float32, 4.5, 6.0)
    values = signs * magnitude
    return values.astype(jnp.float32)


def draw_positions(key, part):
    table = molecule_table(key)
    place_key = jax.random.fold_in(key, 41)
    centre_key, first_key, second_key, noise_key = jax.random.split(place_key, 4)
    centres = jax.random.uniform(centre_key, (CELLS, SLOTS, 3), jnp.float32, 0.05, 0.95)
    cell_rows = jnp.broadcast_to(jnp.arange(CELLS)[:, None], (CELLS, MOLS))
    oxygen_slots = jnp.minimum(table[:, :, 0], SLOTS - 1)
    oxygen_sites = centres[cell_rows, oxygen_slots]
    first_dir = jax.random.normal(first_key, (CELLS, MOLS, 3), jnp.float32)
    first_dir = first_dir / (jnp.sqrt(jnp.sum(first_dir * first_dir, axis=2, keepdims=True)) + 1e-06)
    other_dir = jax.random.normal(second_key, (CELLS, MOLS, 3), jnp.float32)
    other_dir = other_dir - jnp.sum(other_dir * first_dir, axis=2, keepdims=True) * first_dir
    other_dir = other_dir / (jnp.sqrt(jnp.sum(other_dir * other_dir, axis=2, keepdims=True)) + 1e-06)
    second_dir = jnp.cos(1.8239) * first_dir + jnp.sin(1.8239) * other_dir
    first_site = oxygen_sites + 0.09 * first_dir
    second_site = oxygen_sites + 0.09 * second_dir
    centres = centres.at[cell_rows, table[:, :, 1]].set(first_site, mode='drop')
    centres = centres.at[cell_rows, table[:, :, 2]].set(second_site, mode='drop')
    spread = 0.015 * jnp.clip(jax.random.normal(noise_key, (BEADS, CELLS, SLOTS, 3), jnp.float32), -4.0, 4.0)
    sites = jnp.clip(centres[None] + spread, -0.1, 1.1)
    return jnp.transpose(sites, (0, 3, 1, 2)).astype(jnp.float32)


def setup_inputs(seed: int = 0) -> dict:
    arg_keys = jax.random.split(jax.random.key(seed), 4)
    positions = draw_positions(jax.random.fold_in(arg_keys[3], 71), 0)
    momenta = draw_momenta(jax.random.fold_in(arg_keys[3], 71), 0)
    molecules = draw_molecules(jax.random.fold_in(arg_keys[3], 71), 0)
    return {"positions": positions, "momenta": momenta, "molecules": molecules}


charge_oxygen = -0.8476
charge_hydrogen = 0.4238
coulomb_scale = 24.0
coulomb_soft = 0.004
well_depth = 0.02
sigma_square = 0.0841
lennard_soft = 0.04
bond_stiffness = 20000.0
bond_square = 0.0081
angle_stiffness = 5000.0
angle_square = 0.0204
cycle_frequency = 60.0
outer_step = 0.02
inner_step = 0.01

def entry_shifts(reach):
    return [0] + list(range(-reach, 0)) + list(range(1, reach + 1))

def cell_tables(molecules, slot_count):
    slot_ids = jnp.arange(slot_count, dtype=jnp.int32)
    one_hot = (jnp.transpose(molecules, (0, 2, 1))[..., None] == slot_ids).astype(jnp.float32)
    members = lax.optimization_barrier(jnp.sum(one_hot, axis=1))
    oxygen = lax.optimization_barrier(jnp.sum(one_hot[:, 0], axis=1))
    hydrogen = lax.optimization_barrier(jnp.sum(one_hot[:, 1] + one_hot[:, 2], axis=1))
    charges = charge_oxygen * oxygen + charge_hydrogen * hydrogen
    masses = 1.0 + 15.0 * oxygen
    same_molecule = jnp.einsum('cmi,cmj->cij', members, members, precision=lax.Precision.HIGHEST)
    return (one_hot, oxygen, charges, masses, 1.0 - same_molecule)

def mode_tables(beads):
    bead_ids = jnp.arange(beads, dtype=jnp.int32)
    products = bead_ids[:, None] * bead_ids[None, :] % beads
    angles = 2.0 * jnp.pi / beads * products.astype(jnp.float32)
    columns = bead_ids[None, :]
    half_beads = beads // 2
    transform = jnp.where(columns == 0, jnp.sqrt(1.0 / beads), jnp.where(columns < half_beads, jnp.sqrt(2.0 / beads) * jnp.cos(angles), jnp.where(columns == half_beads, jnp.sqrt(1.0 / beads) * jnp.cos(angles), jnp.sqrt(2.0 / beads) * jnp.sin(angles))))
    transform = transform.astype(jnp.float32)
    frequencies = 2.0 * cycle_frequency * jnp.sin(jnp.pi * bead_ids.astype(jnp.float32) / beads)
    cosines = jnp.cos(frequencies * inner_step)
    spring_factor = frequencies * jnp.sin(frequencies * inner_step)
    safe_freq = jnp.where(bead_ids == 0, 1.0, frequencies)
    drift_factor = jnp.where(bead_ids == 0, inner_step, jnp.sin(frequencies * inner_step) / safe_freq)
    return (transform, cosines, spring_factor, drift_factor)

def pair_force(own_atoms, peer_atoms, own_charge, peer_charge, own_oxygen, peer_oxygen, exclusion):
    gap_x = own_atoms[0][:, :, None] - peer_atoms[0][:, None, :]
    gap_y = own_atoms[1][:, :, None] - peer_atoms[1][:, None, :]
    gap_z = own_atoms[2][:, :, None] - peer_atoms[2][:, None, :]
    squares = gap_x * gap_x + gap_y * gap_y + gap_z * gap_z
    charge_pair = own_charge[:, :, None] * peer_charge[:, None, :]
    oxygen_pair = own_oxygen[:, :, None] * peer_oxygen[:, None, :]
    inverse_coulomb = 1.0 / (squares + coulomb_soft)
    coulomb = coulomb_scale * charge_pair * inverse_coulomb * jnp.sqrt(inverse_coulomb)
    inverse_lennard = 1.0 / (squares + lennard_soft)
    sigma_ratio = sigma_square * inverse_lennard
    ratio_cubed = sigma_ratio * sigma_ratio * sigma_ratio
    lennard = 24.0 * well_depth * oxygen_pair * (2.0 * ratio_cubed * ratio_cubed - ratio_cubed) * inverse_lennard
    strength = coulomb + lennard
    if exclusion is not None:
        strength = strength * exclusion
    totals = lax.optimization_barrier(jnp.sum(strength, axis=2))
    weighted = jnp.einsum('nij,knj->kni', strength, peer_atoms, precision=lax.Precision.HIGHEST)
    return own_atoms * totals[None] - weighted

def bond_forces(coords, one_hot):
    parts = jnp.einsum('ctms,bkcs->tbkcm', one_hot, coords, precision=lax.Precision.HIGHEST)
    first_bond = parts[0] - parts[1]
    second_bond = parts[0] - parts[2]
    third_bond = parts[1] - parts[2]
    first_pull = bond_stiffness * (lax.optimization_barrier(jnp.sum(first_bond * first_bond, axis=1, keepdims=True)) - bond_square)
    second_pull = bond_stiffness * (lax.optimization_barrier(jnp.sum(second_bond * second_bond, axis=1, keepdims=True)) - bond_square)
    third_pull = angle_stiffness * (lax.optimization_barrier(jnp.sum(third_bond * third_bond, axis=1, keepdims=True)) - angle_square)
    on_parts = jnp.stack([-first_pull * first_bond - second_pull * second_bond, first_pull * first_bond - third_pull * third_bond, second_pull * second_bond + third_pull * third_bond])
    return jnp.einsum('ctms,tbkcm->bkcs', one_hot, on_parts, precision=lax.Precision.HIGHEST)

def free_polymer(coords, moments, masses, transform, cosines, spring_factor, drift_factor):
    shape = coords.shape
    coord_modes = jnp.dot(transform.T, coords.reshape(shape[0], -1), precision=lax.Precision.HIGHEST).reshape(shape)
    moment_modes = jnp.dot(transform.T, moments.reshape(shape[0], -1), precision=lax.Precision.HIGHEST).reshape(shape)
    weight = masses[None, None]
    cos_col = cosines[:, None, None, None]
    spring_col = spring_factor[:, None, None, None]
    drift_col = drift_factor[:, None, None, None]
    new_moments = cos_col * moment_modes - spring_col * weight * coord_modes
    new_coords = drift_col * moment_modes / weight + cos_col * coord_modes
    coords_out = jnp.dot(transform, new_coords.reshape(shape[0], -1), precision=lax.Precision.HIGHEST).reshape(shape)
    moments_out = jnp.dot(transform, new_moments.reshape(shape[0], -1), precision=lax.Precision.HIGHEST).reshape(shape)
    return (coords_out, moments_out)

def inter_forces(coords, charges, oxygen, exclusion):
    unit_x = jnp.array([1.0, 0.0, 0.0], dtype=jnp.float32)[:, None, None]
    shifts = entry_shifts(REACH)

    def per_cell(cell_index):
        own_atoms = jnp.swapaxes(lax.dynamic_index_in_dim(coords, cell_index, 2, keepdims=False), 0, 1)
        total_force = jnp.zeros_like(own_atoms)
        for entry_index in range(NEIGH):
            shift_cells = shifts[entry_index]
            peer_cell = ((cell_index + shift_cells) % CELLS).astype(jnp.int32)
            peer_atoms = jnp.swapaxes(lax.dynamic_index_in_dim(coords, peer_cell, 2, keepdims=False), 0, 1)
            peer_atoms = peer_atoms + float(shift_cells) * unit_x
            excluded = exclusion[cell_index][None] if entry_index == 0 else None
            total_force = total_force + pair_force(own_atoms, peer_atoms, charges[cell_index][None], charges[peer_cell][None], oxygen[cell_index][None], oxygen[peer_cell][None], excluded)
        return jnp.swapaxes(total_force, 0, 1)
    forces = lax.map(per_cell, jnp.arange(CELLS, dtype=jnp.int32))
    return jnp.transpose(forces, (1, 2, 0, 3))

def reference(positions, momenta, molecules):
    one_hot, oxygen, charges, masses, exclusion = cell_tables(molecules, SLOTS)
    transform, cosines, spring_factor, drift_factor = mode_tables(BEADS)
    coords = positions
    moments = momenta
    outer_force = inter_forces(coords, charges, oxygen, exclusion)
    inner_force = bond_forces(coords, one_hot)
    for outer_index in range(1):
        moments = moments + 0.5 * outer_step * outer_force
        for inner_index in range(2):
            moments = moments + 0.5 * inner_step * inner_force
            coords, moments = free_polymer(coords, moments, masses, transform, cosines, spring_factor, drift_factor)
            inner_force = bond_forces(coords, one_hot)
            moments = moments + 0.5 * inner_step * inner_force
        outer_force = inter_forces(coords, charges, oxygen, exclusion)
        moments = moments + 0.5 * outer_step * outer_force
    return (coords, moments)
```

```python
import functools

import jax
import jax.numpy as jnp
import numpy as np
from jax import lax
from jax.experimental import pallas as pl
from jax.experimental.pallas import tpu as pltpu
from jax.sharding import PartitionSpec as P

MESH = pl.DeviceIdType.MESH

SLOTS = 128
MOLS = 42
CELLS = 16
BEADS = 32
GROUP = 16
SPACE = 32
FLIP = 16

charge_oxygen = -0.8476
charge_hydrogen = 0.4238
coulomb_scale = 24.0
coulomb_soft = 0.004
well_depth = 0.02
sigma_square = 0.0841
lennard_soft = 0.04
bond_stiffness = 20000.0
bond_square = 0.0081
angle_stiffness = 5000.0
angle_square = 0.0204
cycle_frequency = 60.0
outer_step = 0.02
inner_step = 0.01
BIG = 2.0**100

f32 = jnp.float32
bf16 = jnp.bfloat16


def propagators():
    ids = np.arange(BEADS)
    angles = 2.0 * np.pi / BEADS * (ids[:, None] * ids[None, :] % BEADS)
    half = BEADS // 2
    col = ids[None, :]
    transform = np.where(
        col == 0,
        np.sqrt(1.0 / BEADS),
        np.where(
            col < half,
            np.sqrt(2.0 / BEADS) * np.cos(angles),
            np.where(
                col == half,
                np.sqrt(1.0 / BEADS) * np.cos(angles),
                np.sqrt(2.0 / BEADS) * np.sin(angles),
            ),
        ),
    )
    freq = 2.0 * cycle_frequency * np.sin(np.pi * ids / BEADS)
    cosk = np.cos(freq * inner_step)
    springk = freq * np.sin(freq * inner_step)
    driftk = np.where(ids == 0, inner_step, np.sin(freq * inner_step) / np.where(ids == 0, 1.0, freq))
    on = [transform @ np.diag(v) @ transform.T for v in (cosk, driftk, -springk)]
    step = [[on[0], on[1]], [on[2], on[0]]]
    tile = np.zeros((2, 3, BEADS), int)
    plane = np.zeros((2, 3, BEADS), int)
    for kind in range(2):
        for k in range(3):
            for j in range(BEADS):
                tile[kind, k, j] = 128 * kind + 8 * (j // 2) + 4 * (j % 2) + k
                plane[kind, k, j] = 96 * kind + 32 * k + j
    first = np.zeros((192, 256))
    second = np.zeros((256, 192))
    for a in range(2):
        for b in range(2):
            for k in range(3):
                first[np.ix_(plane[a, k], tile[b, k])] = step[a][b]
                second[np.ix_(tile[a, k], plane[b, k])] = step[a][b]
    return first.astype(np.float32), second.astype(np.float32)


def dot(a, b):
    return jnp.dot(a, b, preferred_element_type=f32)


def dot_nt(a, b):
    return lax.dot_general(a, b, (((1,), (1,)), ((), ())), preferred_element_type=f32)


def dot_tn(a, b):
    return lax.dot_general(a, b, (((0,), (0,)), ((), ())), preferred_element_type=f32)


def split2(x):
    high = x.astype(bf16)
    low = (x - high.astype(f32)).astype(bf16)
    return high, low


def split3(x):
    high = x.astype(bf16)
    rest = x - high.astype(f32)
    mid = rest.astype(bf16)
    low = (rest - mid.astype(f32)).astype(bf16)
    return high, mid, low


def parts3(x):
    high, mid, low = split3(x)
    return high.astype(f32), mid.astype(f32), low.astype(f32)


def moved_exactly(rows, hot, product):
    count = rows.shape[0]
    high, mid, low = split3(rows)
    out = product(jnp.concatenate([high, mid, low], axis=0), hot)
    return out[:count] + out[count : 2 * count] + out[2 * count :]


def rolled(x, shift):
    return pltpu.roll(x, shift, 1)


def bonds(planes, used_oxygen):
    one = [rolled(x, SLOTS - MOLS) for x in planes]
    two = [rolled(x, SLOTS - 2 * MOLS) for x in planes]
    d1 = [x - a for x, a in zip(planes, one)]
    d2 = [x - a for x, a in zip(planes, two)]
    d3 = [a - b for a, b in zip(one, two)]
    c1 = bond_stiffness * (d1[0] * d1[0] + d1[1] * d1[1] + d1[2] * d1[2] - bond_square)
    c2 = bond_stiffness * (d2[0] * d2[0] + d2[1] * d2[1] + d2[2] * d2[2] - bond_square)
    c3 = angle_stiffness * (d3[0] * d3[0] + d3[1] * d3[1] + d3[2] * d3[2] - angle_square)
    c1, c2, c3 = c1 * used_oxygen, c2 * used_oxygen, c3 * used_oxygen
    out = []
    for k in range(3):
        a, b, c = c1 * d1[k], c2 * d2[k], c3 * d3[k]
        out.append(rolled(a - c, MOLS) + rolled(b + c, 2 * MOLS) - (a + b))
    return out


def patterns():
    lane = lax.broadcasted_iota(jnp.int32, (1, SLOTS), 1)
    is_oxygen = jnp.where(lane < MOLS, 1.0, 0.0).astype(f32)
    charge = jnp.where(lane < MOLS, charge_oxygen, charge_hydrogen).astype(f32)
    return is_oxygen, charge


def left_features(xyz, row):
    norm = jnp.sum(xyz * xyz, axis=0, keepdims=True)
    full = jnp.where(row == 3, norm + coulomb_soft, jnp.where(row == 4, 1.0, xyz))
    h, m, l = parts3(full)
    return jnp.concatenate([h, h, m, m, h, l], axis=0).astype(bf16)


def right_features(xyz, row):
    norm = jnp.sum(xyz * xyz, axis=0, keepdims=True)
    full = jnp.where(row == 3, 1.0, jnp.where(row == 4, norm, -2.0 * xyz))
    h, m, l = parts3(full)
    return jnp.concatenate([h, m, h, m, l, h], axis=0).astype(bf16)


def sum_features(xyz, row, weight):
    full = jnp.where(row == 3, 1.0, xyz) * weight
    high = full.astype(bf16).astype(f32)
    return jnp.concatenate([high, full - high], axis=0).astype(bf16)


def both(high_low, feats, product):
    high, low = high_low
    out = product(feats, high) + product(feats, low)
    return out[0:8] + out[8:16]


def forces(tile_of, used_of, own_ref, next_ref, mask_ref, lj_mask_ref, first, last):
    is_oxygen, charge = patterns()
    row = lax.broadcasted_iota(jnp.int32, (8, SLOTS), 0)
    lane = lax.broadcasted_iota(jnp.int32, (8, SLOTS), 1)

    def xyz_of(tile, bead, shift):
        tile = tile if bead == 0 else pltpu.roll(tile, 4, 0)
        return jnp.where(row < 3, tile - jnp.where(row == 0, shift, 0.5), 0.0)

    def joined(parts):
        zero, one = parts
        return jnp.where(row < 4, zero, pltpu.roll(one, 4, 0))

    def strength(squares):
        y = lax.rsqrt(squares)
        return split2(y * y * y)

    def pulled(xyz, sums):
        return xyz * sums[3:4, :] - sums

    def beside(c, xyz, left, feats, q):
        tile, q2 = tile_of(c + 1), used_of(c + 1) * charge
        on_c, on_next = [], []
        for bead in range(2):
            xyz2 = xyz_of(tile, bead, -0.5)
            g = strength(dot_tn(left[bead], right_features(xyz2, row)))
            on_c.append(both(g, sum_features(xyz2, row, q2), dot_nt))
            on_next.append(pulled(xyz2, both(g, feats[bead], dot)))
        next_ref[c + 1] = joined(on_next) * (coulomb_scale * q2)
        return on_c

    def own(c, alone):
        tile, used = tile_of(c), used_of(c)
        q = used * charge
        xyz = [xyz_of(tile, bead, 0.5) for bead in range(2)]
        left = [left_features(x, row) for x in xyz]
        feats = [sum_features(x, row, q) for x in xyz]
        sums = beside(c, xyz, left, feats, q)
        if alone:
            return
        before, after = tile_of(c - 1), tile_of(c + 1)
        ox = used * is_oxygen
        ox_lanes = jnp.where(
            lane[:1] < MOLS,
            used_of(c - 1),
            jnp.where(
                lane[:1] < 2 * MOLS,
                rolled(used, MOLS),
                jnp.where(lane[:1] < 3 * MOLS, rolled(used_of(c + 1), 2 * MOLS), 0.0),
            ),
        )
        total = []
        for bead in range(2):
            squares = dot_tn(left[bead], right_features(xyz[bead], row)) + mask_ref[...]
            s = sums[bead] + both(strength(squares), feats[bead], dot)
            force = pulled(xyz[bead], s) * (coulomb_scale * q)
            three = jnp.where(
                lane < MOLS,
                xyz_of(before, bead, 1.5),
                jnp.where(
                    lane < 2 * MOLS,
                    rolled(xyz[bead], MOLS),
                    rolled(xyz_of(after, bead, -0.5), 2 * MOLS),
                ),
            )
            squares = dot_tn(left[bead][:, :48], right_features(three, row)) + lj_mask_ref[...]
            y = lax.rsqrt(squares + (lennard_soft - coulomb_soft))
            ratio = (sigma_square * y) * y
            cubed = ratio * ratio * ratio
            g = (2.0 * cubed * cubed - cubed) * (y * y * (24.0 * well_depth))
            t = both(split2(g), sum_features(three, row, ox_lanes), dot_nt)
            t = jnp.concatenate([t, jnp.zeros((8, SLOTS - 48), f32)], axis=1)
            total.append(force + pulled(xyz[bead], t) * ox)
        own_ref[c] = joined(total)

    own(first - 1, True)

    def body(c, carry):
        own(c, False)
        return carry

    lax.fori_loop(first, last + 1, body, 0)


def kernel(
    pos_ref,
    mom_ref,
    ids_ref,
    first_ref,
    second_ref,
    x_out,
    p_out,
    raw,
    hot,
    tiles,
    moms,
    own_ref,
    next_ref,
    mask_ref,
    lj_mask_ref,
    sent_v,
    mode_in,
    mode_out,
    back_x,
    back_v,
    halo_send,
    halo_recv,
    in_send,
    in_recv,
    out_send,
    out_recv,
    v_recv,
):
    b = lax.axis_index("bead")
    s = lax.axis_index("space")
    far = lax.rem(s + FLIP, SPACE)
    right = lax.rem(s + 1, SPACE)
    left = lax.rem(s + SPACE - 1, SPACE)
    far_right = lax.rem(far + 1, SPACE)
    far_left = lax.rem(far + SPACE - 1, SPACE)

    barrier = pltpu.get_barrier_semaphore()

    def hello(peer, carry):
        pl.semaphore_signal(barrier, inc=1, device_id=(peer, far), device_id_type=MESH)
        return carry

    lax.fori_loop(0, GROUP, hello, 0)
    for who in (
        (b, left),
        (b, right),
        (GROUP - 1, far_left),
        (0, far_right),
    ):
        pl.semaphore_signal(barrier, inc=1, device_id=who, device_id_type=MESH)

    raw[...] = jnp.zeros_like(raw)
    for bead in range(2):
        for k in range(3):
            raw[pl.ds(4 * bead + k, CELLS, stride=16), :] = pos_ref[bead, k]
            raw[pl.ds(8 + 4 * bead + k, CELLS, stride=16), :] = mom_ref[bead, k]

    sub = lax.broadcasted_iota(jnp.int32, (SLOTS, SLOTS), 0)
    lane = lax.broadcasted_iota(jnp.int32, (SLOTS, SLOTS), 1)
    same = (sub % MOLS == lane % MOLS) & (sub < 3 * MOLS) & (lane < 3 * MOLS)
    mask_ref[...] = jnp.where(same, BIG, 0.0).astype(f32)
    lj_mask_ref[...] = jnp.where(lane[:48] == sub[:48] + MOLS, BIG, 0.0).astype(f32)

    ids = ids_ref[...]
    used_all = jnp.where(ids < SLOTS, 1.0, 0.0).astype(f32)
    below = jnp.where(lane < sub, 1.0, 0.0).astype(bf16)
    above = jnp.where(sub < lane, 1.0, 0.0).astype(bf16)
    spare = dot((1.0 - used_all).astype(bf16), above)
    keys = jnp.where(ids < SLOTS, ids.astype(f32), spare + 1000.0)
    ones = jnp.ones((SLOTS, SLOTS), bf16)
    sub_f = sub.astype(f32)
    row16 = lax.broadcasted_iota(jnp.int32, (16, SLOTS), 0)

    for c in range(CELLS):
        key = keys[c : c + 1]
        used = used_all[c : c + 1]
        mine = sub_f == key
        taken = dot(jnp.where(mine, 1.0, 0.0).astype(bf16), ones)
        rank = sub_f - dot(below, taken.astype(bf16))
        spare_key = jnp.where(taken > 0.5, -1.0, rank + 1000.0)
        place = jnp.where(mine | (spare_key == key), 1.0, 0.0).astype(bf16)
        hot[c] = place
        rows = moved_exactly(raw[16 * c : 16 * c + 16], place, dot)
        rows = jnp.where(row16 == 3, used, rows)
        tiles[c + 1] = rows[:8]
        moms[c] = rows[8:]

    pl.semaphore_wait(
        barrier,
        GROUP + 2 + jnp.where(b == 0, GROUP, 0) + jnp.where(b == GROUP - 1, GROUP, 0),
    )

    to_left = pltpu.make_async_remote_copy(
        src_ref=tiles.at[1],
        dst_ref=tiles.at[CELLS + 1],
        send_sem=halo_send.at[0],
        recv_sem=halo_recv.at[0],
        device_id=(b, left),
        device_id_type=MESH,
    )
    to_right = pltpu.make_async_remote_copy(
        src_ref=tiles.at[CELLS],
        dst_ref=tiles.at[0],
        send_sem=halo_send.at[1],
        recv_sem=halo_recv.at[1],
        device_id=(b, right),
        device_id_type=MESH,
    )
    to_left.start()
    to_right.start()

    def send_x(i, carry):
        peer = lax.rem(b + GROUP // 2 + i, GROUP)
        pltpu.make_async_remote_copy(
            src_ref=tiles.at[peer + 1],
            dst_ref=mode_in.at[0, b],
            send_sem=in_send.at[0],
            recv_sem=in_recv.at[0],
            device_id=(peer, far),
            device_id_type=MESH,
        ).start()
        return carry

    lax.fori_loop(0, GROUP, send_x, 0)
    to_left.wait()
    to_right.wait()

    is_oxygen, _ = patterns()
    used_planes = jnp.concatenate([used_all, used_all], axis=0)
    used_ox = used_planes * is_oxygen
    inverse_mass = 1.0 - (15.0 / 16.0) * used_ox
    mass = 1.0 + 15.0 * used_ox

    def used_of(c):
        return tiles[c, 3:4, :]

    tiles_rows = tiles.reshape((CELLS + 2) * 8, SLOTS)
    moms_rows = moms.reshape(CELLS * 8, SLOTS)
    own_rows = own_ref.reshape((CELLS + 2) * 8, SLOTS)
    next_rows = next_ref.reshape((CELLS + 2) * 8, SLOTS)
    sent_rows = sent_v.reshape(CELLS * 8, SLOTS)
    back_x_rows = back_x.reshape((CELLS + 2) * 8, SLOTS)
    back_v_rows = back_v.reshape(CELLS * 8, SLOTS)

    def plane(ref, start, k):
        return jnp.concatenate(
            [ref[pl.ds(start + 4 * bead + k, CELLS, stride=8), :] for bead in range(2)], axis=0
        )

    forces(lambda c: tiles[c], used_of, own_ref, next_ref, mask_ref, lj_mask_ref, 1, CELLS)
    inner = bonds([plane(tiles_rows, 8, k) for k in range(3)], used_ox)
    sent_v[...] = jnp.zeros_like(sent_v)
    for k in range(3):
        outer = plane(own_rows, 8, k) + plane(next_rows, 8, k)
        p = plane(moms_rows, 0, k) + (0.5 * outer_step) * outer
        v = (p + (0.5 * inner_step) * inner[k]) * inverse_mass
        for bead in range(2):
            sent_rows[pl.ds(4 * bead + k, CELLS, stride=8), :] = v[CELLS * bead : CELLS * bead + CELLS]

    def send_v(i, carry):
        peer = lax.rem(b + GROUP // 2 + i, GROUP)
        pltpu.make_async_remote_copy(
            src_ref=sent_v.at[peer],
            dst_ref=mode_in.at[1, b],
            send_sem=in_send.at[1],
            recv_sem=in_recv.at[1],
            device_id=(peer, far),
            device_id_type=MESH,
        ).start()
        return carry

    lax.fori_loop(0, GROUP, send_v, 0)

    def all_of(kind, ref, send_sem, recv_sem):
        return pltpu.make_async_remote_copy(
            src_ref=ref,
            dst_ref=mode_in.at[kind],
            send_sem=send_sem,
            recv_sem=recv_sem,
            device_id=(b, far),
            device_id_type=MESH,
        )

    all_of(0, tiles.at[pl.ds(1, CELLS)], in_send.at[0], in_recv.at[0]).wait()
    all_of(1, sent_v, in_send.at[1], in_recv.at[1]).wait()

    mode_rows = mode_in[...].reshape(256, SLOTS)
    mode_ox = mode_in[0, 0, 3:4, :] * is_oxygen
    mode_inverse = 1.0 - (15.0 / 16.0) * mode_ox
    evolved = jnp.dot(first_ref[...], mode_rows, precision=lax.Precision.HIGHEST, preferred_element_type=f32)
    pull = bonds([evolved[32 * k : 32 * k + 32] for k in range(3)], mode_ox)
    kicked = [evolved[96 + 32 * k : 128 + 32 * k] + (inner_step * mode_inverse) * pull[k] for k in range(3)]
    state = jnp.concatenate([evolved[:96], *kicked], axis=0)
    mode_out[...] = jnp.dot(
        second_ref[...], state, precision=lax.Precision.HIGHEST, preferred_element_type=f32
    ).reshape(2, GROUP, 8, SLOTS)

    def back(kind, src, dst, group, recv_sem):
        def send(i, carry):
            peer = lax.rem(b + GROUP // 2 + i, GROUP)
            pltpu.make_async_remote_copy(
                src_ref=mode_out.at[kind, peer],
                dst_ref=dst,
                send_sem=out_send.at[src],
                recv_sem=recv_sem,
                device_id=(peer, group),
                device_id_type=MESH,
            ).start()
            return carry

        lax.fori_loop(0, GROUP, send, 0)

    back(0, 0, back_x.at[b + 1], far, out_recv.at[b + 1])

    @pl.when(b == 0)
    def _():
        back(0, 2, back_x.at[CELLS + 1], far_left, out_recv.at[CELLS + 1])

    @pl.when(b == GROUP - 1)
    def _():
        back(0, 2, back_x.at[0], far_right, out_recv.at[0])

    back(1, 1, back_v.at[b], far, v_recv)

    for c in range(CELLS + 2):
        pltpu.make_async_copy(back_x.at[c], back_x.at[c], out_recv.at[c]).wait()

    forces(lambda c: back_x[c], used_of, own_ref, next_ref, mask_ref, lj_mask_ref, 1, CELLS)
    inner = bonds([plane(back_x_rows, 8, k) for k in range(3)], used_ox)
    pltpu.make_async_copy(back_v, back_v, v_recv).wait()
    for k in range(3):
        outer = plane(own_rows, 8, k) + plane(next_rows, 8, k)
        p = mass * plane(back_v_rows, 0, k) + (0.5 * inner_step) * inner[k]
        p = p + (0.5 * outer_step) * outer
        x = plane(back_x_rows, 8, k)
        for bead in range(2):
            half = slice(CELLS * bead, CELLS * bead + CELLS)
            raw[pl.ds(4 * bead + k, CELLS, stride=16), :] = x[half]
            raw[pl.ds(8 + 4 * bead + k, CELLS, stride=16), :] = p[half]
    for c in range(CELLS):
        raw[16 * c : 16 * c + 16] = moved_exactly(raw[16 * c : 16 * c + 16], hot[c], dot_nt)
    for bead in range(2):
        for k in range(3):
            x_out[bead, k] = raw[pl.ds(4 * bead + k, CELLS, stride=16), :]
            p_out[bead, k] = raw[pl.ds(8 + 4 * bead + k, CELLS, stride=16), :]

    pltpu.make_async_copy(mode_out.at[0], mode_out.at[0], out_send.at[0]).wait()
    pltpu.make_async_copy(mode_out.at[1], mode_out.at[1], out_send.at[1]).wait()

    @pl.when((b == 0) | (b == GROUP - 1))
    def _():
        pltpu.make_async_copy(mode_out.at[0], mode_out.at[0], out_send.at[2]).wait()


def local(positions, momenta, molecules):
    ids = jnp.transpose(molecules, (0, 2, 1)).reshape(CELLS, 3 * MOLS)
    ids = jnp.pad(ids, ((0, 0), (0, SLOTS - 3 * MOLS)), constant_values=SLOTS)
    first, second = propagators()
    vmem = pl.BlockSpec(memory_space=pltpu.VMEM)
    return pl.pallas_call(
        kernel,
        out_shape=[jax.ShapeDtypeStruct(positions.shape, f32)] * 2,
        in_specs=[vmem] * 5,
        out_specs=[vmem] * 2,
        scratch_shapes=[
            pltpu.VMEM((CELLS * 16, SLOTS), f32),
            pltpu.VMEM((CELLS, SLOTS, SLOTS), bf16),
            pltpu.VMEM((CELLS + 2, 8, SLOTS), f32),
            pltpu.VMEM((CELLS, 8, SLOTS), f32),
            pltpu.VMEM((CELLS + 2, 8, SLOTS), f32),
            pltpu.VMEM((CELLS + 2, 8, SLOTS), f32),
            pltpu.VMEM((SLOTS, SLOTS), f32),
            pltpu.VMEM((48, SLOTS), f32),
            pltpu.VMEM((CELLS, 8, SLOTS), f32),
            pltpu.VMEM((2, GROUP, 8, SLOTS), f32),
            pltpu.VMEM((2, GROUP, 8, SLOTS), f32),
            pltpu.VMEM((CELLS + 2, 8, SLOTS), f32),
            pltpu.VMEM((CELLS, 8, SLOTS), f32),
            pltpu.SemaphoreType.DMA((2,)),
            pltpu.SemaphoreType.DMA((2,)),
            pltpu.SemaphoreType.DMA((2,)),
            pltpu.SemaphoreType.DMA((2,)),
            pltpu.SemaphoreType.DMA((3,)),
            pltpu.SemaphoreType.DMA((CELLS + 2,)),
            pltpu.SemaphoreType.DMA,
        ],
        compiler_params=pltpu.CompilerParams(collective_id=0, has_side_effects=True),
    )(positions, momenta, ids, jnp.asarray(first), jnp.asarray(second))


def solution(mesh):
    wide = P("bead", None, "space", None)
    return jax.shard_map(
        local,
        mesh=mesh,
        in_specs=(wide, wide, P("space", None, None)),
        out_specs=(wide, wide),
        check_vma=False,
    )
```

```python
import functools

import jax
import jax.numpy as jnp
import numpy as np
from jax import lax
from jax.experimental import pallas as pl
from jax.experimental.pallas import tpu as pltpu
from jax.sharding import PartitionSpec as P

MESH = pl.DeviceIdType.MESH

SLOTS = 128
MOLS = 42
CELLS = 16
BEADS = 32
GROUP = 16
SPACE = 32
FLIP = 16

charge_oxygen = -0.8476
charge_hydrogen = 0.4238
coulomb_scale = 24.0
coulomb_soft = 0.004
well_depth = 0.02
sigma_square = 0.0841
lennard_soft = 0.04
bond_stiffness = 20000.0
bond_square = 0.0081
angle_stiffness = 5000.0
angle_square = 0.0204
cycle_frequency = 60.0
outer_step = 0.02
inner_step = 0.01
BIG = 2.0**100

f32 = jnp.float32
bf16 = jnp.bfloat16


def propagators():
    ids = np.arange(BEADS)
    angles = 2.0 * np.pi / BEADS * (ids[:, None] * ids[None, :] % BEADS)
    half = BEADS // 2
    col = ids[None, :]
    transform = np.where(
        col == 0,
        np.sqrt(1.0 / BEADS),
        np.where(
            col < half,
            np.sqrt(2.0 / BEADS) * np.cos(angles),
            np.where(
                col == half,
                np.sqrt(1.0 / BEADS) * np.cos(angles),
                np.sqrt(2.0 / BEADS) * np.sin(angles),
            ),
        ),
    )
    freq = 2.0 * cycle_frequency * np.sin(np.pi * ids / BEADS)
    cosk = np.cos(freq * inner_step)
    springk = freq * np.sin(freq * inner_step)
    driftk = np.where(ids == 0, inner_step, np.sin(freq * inner_step) / np.where(ids == 0, 1.0, freq))
    on = [transform @ np.diag(v) @ transform.T for v in (cosk, driftk, -springk)]
    step = [[on[0], on[1]], [on[2], on[0]]]
    tile = np.zeros((2, 3, BEADS), int)
    plane = np.zeros((2, 3, BEADS), int)
    for kind in range(2):
        for k in range(3):
            for j in range(BEADS):
                tile[kind, k, j] = 128 * kind + 8 * (j // 2) + 4 * (j % 2) + k
                plane[kind, k, j] = 96 * kind + 32 * k + j
    first = np.zeros((192, 256))
    second = np.zeros((256, 192))
    for a in range(2):
        for b in range(2):
            for k in range(3):
                first[np.ix_(plane[a, k], tile[b, k])] = step[a][b]
                second[np.ix_(tile[a, k], plane[b, k])] = step[a][b]
    return first.astype(np.float32), second.astype(np.float32)


def dot(a, b):
    return jnp.dot(a, b, preferred_element_type=f32)


def dot_nt(a, b):
    return lax.dot_general(a, b, (((1,), (1,)), ((), ())), preferred_element_type=f32)


def split2(x):
    high = x.astype(bf16)
    low = (x - high.astype(f32)).astype(bf16)
    return high, low


def split3(x):
    high = x.astype(bf16)
    rest = x - high.astype(f32)
    mid = rest.astype(bf16)
    low = (rest - mid.astype(f32)).astype(bf16)
    return high, mid, low


def parts3(x):
    high, mid, low = split3(x)
    return high.astype(f32), mid.astype(f32), low.astype(f32)


def moved_exactly(rows, hot, product):
    count = rows.shape[0]
    high, mid, low = split3(rows)
    out = product(jnp.concatenate([high, mid, low], axis=0), hot)
    return out[:count] + out[count : 2 * count] + out[2 * count :]


def rolled(x, shift):
    return pltpu.roll(x, shift, 1)


def bonds(planes, used_oxygen):
    one = [rolled(x, SLOTS - MOLS) for x in planes]
    two = [rolled(x, SLOTS - 2 * MOLS) for x in planes]
    d1 = [x - a for x, a in zip(planes, one)]
    d2 = [x - a for x, a in zip(planes, two)]
    d3 = [a - b for a, b in zip(one, two)]
    c1 = bond_stiffness * (d1[0] * d1[0] + d1[1] * d1[1] + d1[2] * d1[2] - bond_square)
    c2 = bond_stiffness * (d2[0] * d2[0] + d2[1] * d2[1] + d2[2] * d2[2] - bond_square)
    c3 = angle_stiffness * (d3[0] * d3[0] + d3[1] * d3[1] + d3[2] * d3[2] - angle_square)
    c1, c2, c3 = c1 * used_oxygen, c2 * used_oxygen, c3 * used_oxygen
    out = []
    for k in range(3):
        a, b, c = c1 * d1[k], c2 * d2[k], c3 * d3[k]
        out.append(rolled(a - c, MOLS) + rolled(b + c, 2 * MOLS) - (a + b))
    return out


def patterns():
    lane = lax.broadcasted_iota(jnp.int32, (1, SLOTS), 1)
    is_oxygen = jnp.where(lane < MOLS, 1.0, 0.0).astype(f32)
    charge = jnp.where(lane < MOLS, charge_oxygen, charge_hydrogen).astype(f32)
    return is_oxygen, charge


def bead_rows(bead):
    row = lax.broadcasted_iota(jnp.int32, (8, SLOTS), 0)
    return (row >= 4 * bead) & (row < 4 * bead + 3), row == 4 * bead + 3, row == (4 * bead + 4) % 8


def left_features(xyz, norm, rows):
    _, is_norm, is_one = rows
    full = jnp.where(is_norm, norm + coulomb_soft, jnp.where(is_one, 1.0, xyz))
    h, m, l = parts3(full)
    return jnp.concatenate([h, h, m, m, h, l], axis=0).astype(bf16)


def right_features(xyz, norm, rows):
    _, is_norm, is_one = rows
    full = jnp.where(is_norm, 1.0, jnp.where(is_one, norm, -2.0 * xyz))
    h, m, l = parts3(full)
    return jnp.concatenate([h, m, h, m, l, h], axis=0).astype(bf16)


def sum_features(xyz, rows, weight):
    full = jnp.where(rows[1], 1.0, xyz) * weight
    high = full.astype(bf16).astype(f32)
    return jnp.concatenate([high, full - high], axis=0).astype(bf16)


def squared(xyz):
    return jnp.sum(xyz * xyz, axis=0, keepdims=True)


def pulled(xyz, sums, bead):
    return xyz * sums[4 * bead + 3 : 4 * bead + 4, :] - sums


def folded(out):
    return out[0:8] + out[8:16]


CHUNK = 32


class Forces:
    def __init__(self, tile_of, used_of, own_ref, next_ref, mask_ref, lj_mask_ref, near_ref, ox_ref, feats_ref, ox_feats_ref):
        self.tile_of, self.used_of, self.own_ref, self.next_ref = tile_of, used_of, own_ref, next_ref
        self.mask_ref, self.lj_mask_ref, self.near_ref, self.ox_ref = mask_ref, lj_mask_ref, near_ref, ox_ref
        self.feats_ref, self.ox_feats_ref = feats_ref, ox_feats_ref
        self.is_oxygen, self.charge = patterns()
        self.rows = [bead_rows(bead) for bead in range(2)]
        self.row = lax.broadcasted_iota(jnp.int32, (8, SLOTS), 0)
        self.lane = lax.broadcasted_iota(jnp.int32, (8, SLOTS), 1)

    def xyz(self, c, bead, cell_shift):
        shift = jnp.where(self.row == 4 * bead, 0.5 - cell_shift, 0.5)
        return jnp.where(self.rows[bead][0], self.tile_of(c) - shift, 0.0)

    def squares(self, c, bead, alone=False):
        rows, lane = self.rows[bead], self.lane
        used, used2 = self.used_of(c), self.used_of(c + 1)
        xyz, xyz2 = self.xyz(c, bead, 0.0), self.xyz(c + 1, bead, 1.0)
        norm, norm2 = squared(xyz), squared(xyz2)
        left = left_features(xyz, norm, rows).T
        right2 = right_features(xyz2, norm2, rows)
        feats = sum_features(xyz, rows, used * self.charge)
        feats2 = sum_features(xyz2, rows, used2 * self.charge)
        self.feats_ref[bead] = jnp.concatenate([feats, feats2], axis=1)
        if alone:
            self.near_ref[bead, :, SLOTS:] = dot(left, right2)
            return
        right = jnp.concatenate([right_features(xyz, norm, rows), right2], axis=1)
        self.near_ref[bead] = dot(left, right)
        used0, xyz0 = self.used_of(c - 1), self.xyz(c - 1, bead, -1.0)
        three = jnp.where(
            lane < MOLS,
            xyz0,
            jnp.where(lane < 2 * MOLS, rolled(xyz, MOLS), rolled(xyz2, 2 * MOLS)),
        )
        ox = jnp.where(
            lane[:1] < MOLS,
            used0,
            jnp.where(
                lane[:1] < 2 * MOLS,
                rolled(used, MOLS),
                jnp.where(lane[:1] < 3 * MOLS, rolled(used2, 2 * MOLS), 0.0),
            ),
        )
        right = right_features(three, squared(three) + (lennard_soft - coulomb_soft), rows)
        self.ox_ref[bead] = dot(left[:48], right)
        self.ox_feats_ref[bead] = sum_features(three, rows, ox)

    def next_sums(self, c, bead, g):
        xyz2 = self.xyz(c + 1, bead, 1.0)
        feats = self.feats_ref[bead, :, :SLOTS]
        sums = folded(dot(feats, g[0]) + dot(feats, g[1]))
        return pulled(xyz2, sums, bead) * (coulomb_scale * self.used_of(c + 1) * self.charge)

    def sums(self, c, bead):
        high, low = [], []
        for i in range(0, SLOTS, CHUNK):
            part = self.near_ref[bead, i : i + CHUNK]
            part = jnp.concatenate([part[:, :SLOTS] + self.mask_ref[i : i + CHUNK], part[:, SLOTS:]], axis=1)
            y = lax.rsqrt(part)
            h, l = split2(y * y * y)
            high.append(h)
            low.append(l)
        high, low = jnp.concatenate(high, axis=0), jnp.concatenate(low, axis=0)
        y = lax.rsqrt(self.ox_ref[bead] + self.lj_mask_ref[...])
        inverse = y * y
        cubed = (inverse * inverse) * (inverse * sigma_square**3)
        g = cubed * (cubed * (48.0 * well_depth) - 24.0 * well_depth) * inverse
        ox_high, ox_low = split2(g)
        xyz = self.xyz(c, bead, 0.0)
        used = self.used_of(c)
        feats = self.feats_ref[bead]
        near = folded(dot_nt(feats, high) + dot_nt(feats, low))
        after = self.next_sums(c, bead, (high[:, SLOTS:], low[:, SLOTS:]))
        ox_feats = self.ox_feats_ref[bead]
        ox = folded(dot_nt(ox_feats, ox_high) + dot_nt(ox_feats, ox_low))
        ox = jnp.concatenate([ox, jnp.zeros((8, SLOTS - 48), f32)], axis=1)
        force = pulled(xyz, near, bead) * (coulomb_scale * used * self.charge)
        return force + pulled(xyz, ox, bead) * (used * self.is_oxygen), after

    def first_halo(self):
        out = []
        for bead in range(2):
            self.squares(0, bead, alone=True)
        for bead in range(2):
            y = lax.rsqrt(self.near_ref[bead, :, SLOTS:])
            out.append(self.next_sums(0, bead, split2(y * y * y)))
        self.next_ref[1] = jnp.where(self.row < 4, out[0], out[1])

    def cells(self, cell_of, count):
        self.squares(cell_of(0), 0)

        def body(i, carry):
            c = cell_of(i)
            self.squares(c, 1)
            near0, after0 = self.sums(c, 0)
            self.squares(cell_of(jnp.minimum(i + 1, count - 1)), 0)
            near1, after1 = self.sums(c, 1)
            self.own_ref[c] = jnp.where(self.row < 4, near0, near1)
            self.next_ref[c + 1] = jnp.where(self.row < 4, after0, after1)
            return carry

        lax.fori_loop(0, count, body, 0)


def kernel(
    pos_ref,
    mom_ref,
    ids_ref,
    first_ref,
    second_ref,
    x_out,
    p_out,
    raw,
    hot,
    tiles,
    moms,
    own_ref,
    next_ref,
    mask_ref,
    lj_mask_ref,
    near_ref,
    ox_ref,
    feats_ref,
    ox_feats_ref,
    sent_v,
    mode_in,
    mode_out,
    back_x,
    back_v,
    halo_send,
    halo_recv,
    in_send,
    in_recv,
    out_send,
    out_recv,
    v_recv,
):
    b = lax.axis_index("bead")
    s = lax.axis_index("space")
    far = lax.rem(s + FLIP, SPACE)
    right = lax.rem(s + 1, SPACE)
    left = lax.rem(s + SPACE - 1, SPACE)
    far_right = lax.rem(far + 1, SPACE)
    far_left = lax.rem(far + SPACE - 1, SPACE)

    barrier = pltpu.get_barrier_semaphore()

    def hello(peer, carry):
        pl.semaphore_signal(barrier, inc=1, device_id=(peer, far), device_id_type=MESH)
        return carry

    lax.fori_loop(0, GROUP, hello, 0)
    for who in (
        (b, left),
        (b, right),
        (GROUP - 1, far_left),
        (0, far_right),
    ):
        pl.semaphore_signal(barrier, inc=1, device_id=who, device_id_type=MESH)

    raw[...] = jnp.zeros_like(raw)
    for bead in range(2):
        for k in range(3):
            raw[pl.ds(4 * bead + k, CELLS, stride=16), :] = pos_ref[bead, k]
            raw[pl.ds(8 + 4 * bead + k, CELLS, stride=16), :] = mom_ref[bead, k]

    sub = lax.broadcasted_iota(jnp.int32, (SLOTS, SLOTS), 0)
    lane = lax.broadcasted_iota(jnp.int32, (SLOTS, SLOTS), 1)
    same = (sub % MOLS == lane % MOLS) & (sub < 3 * MOLS) & (lane < 3 * MOLS)
    mask_ref[...] = jnp.where(same, BIG, 0.0).astype(f32)
    lj_mask_ref[...] = jnp.where(lane[:48] == sub[:48] + MOLS, BIG, 0.0).astype(f32)

    ids = ids_ref[...]
    used_all = jnp.where(ids < SLOTS, 1.0, 0.0).astype(f32)
    below = jnp.where(lane < sub, 1.0, 0.0).astype(bf16)
    above = jnp.where(sub < lane, 1.0, 0.0).astype(bf16)
    spare = dot((1.0 - used_all).astype(bf16), above)
    keys = jnp.where(ids < SLOTS, ids.astype(f32), spare + 1000.0)
    ones = jnp.ones((SLOTS, SLOTS), bf16)
    sub_f = sub.astype(f32)
    row16 = lax.broadcasted_iota(jnp.int32, (16, SLOTS), 0)

    for c in range(CELLS):
        key = keys[c : c + 1]
        used = used_all[c : c + 1]
        mine = sub_f == key
        taken = dot(jnp.where(mine, 1.0, 0.0).astype(bf16), ones)
        rank = sub_f - dot(below, taken.astype(bf16))
        spare_key = jnp.where(taken > 0.5, -1.0, rank + 1000.0)
        place = jnp.where(mine | (spare_key == key), 1.0, 0.0).astype(bf16)
        hot[c] = place
        rows = moved_exactly(raw[16 * c : 16 * c + 16], place, dot)
        rows = jnp.where(row16 == 3, used, rows)
        tiles[c + 1] = rows[:8]
        moms[c] = rows[8:]

    pl.semaphore_wait(
        barrier,
        GROUP + 2 + jnp.where(b == 0, GROUP, 0) + jnp.where(b == GROUP - 1, GROUP, 0),
    )

    to_left = pltpu.make_async_remote_copy(
        src_ref=tiles.at[1],
        dst_ref=tiles.at[CELLS + 1],
        send_sem=halo_send.at[0],
        recv_sem=halo_recv.at[0],
        device_id=(b, left),
        device_id_type=MESH,
    )
    to_right = pltpu.make_async_remote_copy(
        src_ref=tiles.at[CELLS],
        dst_ref=tiles.at[0],
        send_sem=halo_send.at[1],
        recv_sem=halo_recv.at[1],
        device_id=(b, right),
        device_id_type=MESH,
    )
    to_left.start()
    to_right.start()

    def send_x(i, carry):
        peer = lax.rem(b + GROUP // 2 + i, GROUP)
        pltpu.make_async_remote_copy(
            src_ref=tiles.at[peer + 1],
            dst_ref=mode_in.at[0, b],
            send_sem=in_send.at[0],
            recv_sem=in_recv.at[0],
            device_id=(peer, far),
            device_id_type=MESH,
        ).start()
        return carry

    lax.fori_loop(0, GROUP, send_x, 0)

    is_oxygen, _ = patterns()
    used_planes = jnp.concatenate([used_all, used_all], axis=0)
    used_ox = used_planes * is_oxygen
    inverse_mass = 1.0 - (15.0 / 16.0) * used_ox
    mass = 1.0 + 15.0 * used_ox

    def used_of(c):
        return tiles[c, 3:4, :]

    tiles_rows = tiles.reshape((CELLS + 2) * 8, SLOTS)
    moms_rows = moms.reshape(CELLS * 8, SLOTS)
    own_rows = own_ref.reshape((CELLS + 2) * 8, SLOTS)
    next_rows = next_ref.reshape((CELLS + 2) * 8, SLOTS)
    sent_rows = sent_v.reshape(CELLS * 8, SLOTS)
    back_x_rows = back_x.reshape((CELLS + 2) * 8, SLOTS)
    back_v_rows = back_v.reshape(CELLS * 8, SLOTS)

    def plane(ref, start, k):
        return jnp.concatenate(
            [ref[pl.ds(start + 4 * bead + k, CELLS, stride=8), :] for bead in range(2)], axis=0
        )

    scratch = (own_ref, next_ref, mask_ref, lj_mask_ref, near_ref, ox_ref, feats_ref, ox_feats_ref)
    now = Forces(lambda c: tiles[c], used_of, *scratch)
    now.cells(lambda i: i + 2, CELLS - 2)
    to_left.wait()
    to_right.wait()
    now.cells(lambda i: CELLS - (CELLS - 1) * i, 2)
    now.first_halo()
    inner = bonds([plane(tiles_rows, 8, k) for k in range(3)], used_ox)
    sent_v[...] = jnp.zeros_like(sent_v)
    for k in range(3):
        outer = plane(own_rows, 8, k) + plane(next_rows, 8, k)
        p = plane(moms_rows, 0, k) + (0.5 * outer_step) * outer
        v = (p + (0.5 * inner_step) * inner[k]) * inverse_mass
        for bead in range(2):
            sent_rows[pl.ds(4 * bead + k, CELLS, stride=8), :] = v[CELLS * bead : CELLS * bead + CELLS]

    def send_v(i, carry):
        peer = lax.rem(b + GROUP // 2 + i, GROUP)
        pltpu.make_async_remote_copy(
            src_ref=sent_v.at[peer],
            dst_ref=mode_in.at[1, b],
            send_sem=in_send.at[1],
            recv_sem=in_recv.at[1],
            device_id=(peer, far),
            device_id_type=MESH,
        ).start()
        return carry

    lax.fori_loop(0, GROUP, send_v, 0)

    def all_of(kind, ref, send_sem, recv_sem):
        return pltpu.make_async_remote_copy(
            src_ref=ref,
            dst_ref=mode_in.at[kind],
            send_sem=send_sem,
            recv_sem=recv_sem,
            device_id=(b, far),
            device_id_type=MESH,
        )

    all_of(0, tiles.at[pl.ds(1, CELLS)], in_send.at[0], in_recv.at[0]).wait()
    all_of(1, sent_v, in_send.at[1], in_recv.at[1]).wait()

    mode_rows = mode_in[...].reshape(256, SLOTS)
    mode_ox = mode_in[0, 0, 3:4, :] * is_oxygen
    mode_inverse = 1.0 - (15.0 / 16.0) * mode_ox
    evolved = jnp.dot(first_ref[...], mode_rows, precision=lax.Precision.HIGHEST, preferred_element_type=f32)
    pull = bonds([evolved[32 * k : 32 * k + 32] for k in range(3)], mode_ox)
    kicked = [evolved[96 + 32 * k : 128 + 32 * k] + (inner_step * mode_inverse) * pull[k] for k in range(3)]
    state = jnp.concatenate([evolved[:96], *kicked], axis=0)
    mode_out[...] = jnp.dot(
        second_ref[...], state, precision=lax.Precision.HIGHEST, preferred_element_type=f32
    ).reshape(2, GROUP, 8, SLOTS)

    def back(kind, src, dst, group, recv_sem):
        def send(i, carry):
            peer = lax.rem(b + GROUP // 2 + i, GROUP)
            pltpu.make_async_remote_copy(
                src_ref=mode_out.at[kind, peer],
                dst_ref=dst,
                send_sem=out_send.at[src],
                recv_sem=recv_sem,
                device_id=(peer, group),
                device_id_type=MESH,
            ).start()
            return carry

        lax.fori_loop(0, GROUP, send, 0)

    back(0, 0, back_x.at[b + 1], far, out_recv.at[b + 1])

    @pl.when(b == 0)
    def _():
        back(0, 2, back_x.at[CELLS + 1], far_left, out_recv.at[CELLS + 1])

    @pl.when(b == GROUP - 1)
    def _():
        back(0, 2, back_x.at[0], far_right, out_recv.at[0])

    back(1, 1, back_v.at[b], far, v_recv)

    for c in range(CELLS + 2):
        pltpu.make_async_copy(back_x.at[c], back_x.at[c], out_recv.at[c]).wait()

    then = Forces(lambda c: back_x[c], used_of, *scratch)
    then.cells(lambda i: i + 1, CELLS)
    then.first_halo()
    inner = bonds([plane(back_x_rows, 8, k) for k in range(3)], used_ox)
    pltpu.make_async_copy(back_v, back_v, v_recv).wait()
    for k in range(3):
        outer = plane(own_rows, 8, k) + plane(next_rows, 8, k)
        p = mass * plane(back_v_rows, 0, k) + (0.5 * inner_step) * inner[k]
        p = p + (0.5 * outer_step) * outer
        x = plane(back_x_rows, 8, k)
        for bead in range(2):
            half = slice(CELLS * bead, CELLS * bead + CELLS)
            raw[pl.ds(4 * bead + k, CELLS, stride=16), :] = x[half]
            raw[pl.ds(8 + 4 * bead + k, CELLS, stride=16), :] = p[half]
    for c in range(CELLS):
        raw[16 * c : 16 * c + 16] = moved_exactly(raw[16 * c : 16 * c + 16], hot[c], dot_nt)
    for bead in range(2):
        for k in range(3):
            x_out[bead, k] = raw[pl.ds(4 * bead + k, CELLS, stride=16), :]
            p_out[bead, k] = raw[pl.ds(8 + 4 * bead + k, CELLS, stride=16), :]

    pltpu.make_async_copy(mode_out.at[0], mode_out.at[0], out_send.at[0]).wait()
    pltpu.make_async_copy(mode_out.at[1], mode_out.at[1], out_send.at[1]).wait()

    @pl.when((b == 0) | (b == GROUP - 1))
    def _():
        pltpu.make_async_copy(mode_out.at[0], mode_out.at[0], out_send.at[2]).wait()


def local(positions, momenta, molecules):
    ids = jnp.transpose(molecules, (0, 2, 1)).reshape(CELLS, 3 * MOLS)
    ids = jnp.pad(ids, ((0, 0), (0, SLOTS - 3 * MOLS)), constant_values=SLOTS)
    first, second = propagators()
    vmem = pl.BlockSpec(memory_space=pltpu.VMEM)
    return pl.pallas_call(
        kernel,
        out_shape=[jax.ShapeDtypeStruct(positions.shape, f32)] * 2,
        in_specs=[vmem] * 5,
        out_specs=[vmem] * 2,
        scratch_shapes=[
            pltpu.VMEM((CELLS * 16, SLOTS), f32),
            pltpu.VMEM((CELLS, SLOTS, SLOTS), bf16),
            pltpu.VMEM((CELLS + 2, 8, SLOTS), f32),
            pltpu.VMEM((CELLS, 8, SLOTS), f32),
            pltpu.VMEM((CELLS + 2, 8, SLOTS), f32),
            pltpu.VMEM((CELLS + 2, 8, SLOTS), f32),
            pltpu.VMEM((SLOTS, SLOTS), f32),
            pltpu.VMEM((48, SLOTS), f32),
            pltpu.VMEM((2, SLOTS, 2 * SLOTS), f32),
            pltpu.VMEM((2, 48, SLOTS), f32),
            pltpu.VMEM((2, 16, 2 * SLOTS), bf16),
            pltpu.VMEM((2, 16, SLOTS), bf16),
            pltpu.VMEM((CELLS, 8, SLOTS), f32),
            pltpu.VMEM((2, GROUP, 8, SLOTS), f32),
            pltpu.VMEM((2, GROUP, 8, SLOTS), f32),
            pltpu.VMEM((CELLS + 2, 8, SLOTS), f32),
            pltpu.VMEM((CELLS, 8, SLOTS), f32),
            pltpu.SemaphoreType.DMA((2,)),
            pltpu.SemaphoreType.DMA((2,)),
            pltpu.SemaphoreType.DMA((2,)),
            pltpu.SemaphoreType.DMA((2,)),
            pltpu.SemaphoreType.DMA((3,)),
            pltpu.SemaphoreType.DMA((CELLS + 2,)),
            pltpu.SemaphoreType.DMA,
        ],
        compiler_params=pltpu.CompilerParams(collective_id=0, has_side_effects=True),
    )(positions, momenta, ids, jnp.asarray(first), jnp.asarray(second))


def solution(mesh):
    wide = P("bead", None, "space", None)
    return jax.shard_map(
        local,
        mesh=mesh,
        in_specs=(wide, wide, P("space", None, None)),
        out_specs=(wide, wide),
        check_vma=False,
    )
```

```python
import functools

import jax
import jax.numpy as jnp
import numpy as np
from jax import lax
from jax.experimental import pallas as pl
from jax.experimental.pallas import tpu as pltpu
from jax.sharding import PartitionSpec as P

MESH = pl.DeviceIdType.MESH

SLOTS = 128
MOLS = 42
CELLS = 16
BEADS = 32
GROUP = 16
SPACE = 32
FLIP = 16

charge_oxygen = -0.8476
charge_hydrogen = 0.4238
coulomb_scale = 24.0
coulomb_soft = 0.004
well_depth = 0.02
sigma_square = 0.0841
lennard_soft = 0.04
bond_stiffness = 20000.0
bond_square = 0.0081
angle_stiffness = 5000.0
angle_square = 0.0204
cycle_frequency = 60.0
outer_step = 0.02
inner_step = 0.01
BIG = 2.0**100

f32 = jnp.float32
bf16 = jnp.bfloat16


def propagators():
    ids = np.arange(BEADS)
    angles = 2.0 * np.pi / BEADS * (ids[:, None] * ids[None, :] % BEADS)
    half = BEADS // 2
    col = ids[None, :]
    transform = np.where(
        col == 0,
        np.sqrt(1.0 / BEADS),
        np.where(
            col < half,
            np.sqrt(2.0 / BEADS) * np.cos(angles),
            np.where(
                col == half,
                np.sqrt(1.0 / BEADS) * np.cos(angles),
                np.sqrt(2.0 / BEADS) * np.sin(angles),
            ),
        ),
    )
    freq = 2.0 * cycle_frequency * np.sin(np.pi * ids / BEADS)
    cosk = np.cos(freq * inner_step)
    springk = freq * np.sin(freq * inner_step)
    driftk = np.where(ids == 0, inner_step, np.sin(freq * inner_step) / np.where(ids == 0, 1.0, freq))
    on = [transform @ np.diag(v) @ transform.T for v in (cosk, driftk, -springk)]
    step = [[on[0], on[1]], [on[2], on[0]]]
    tile = np.zeros((2, 3, BEADS), int)
    plane = np.zeros((2, 3, BEADS), int)
    for kind in range(2):
        for k in range(3):
            for j in range(BEADS):
                tile[kind, k, j] = 128 * kind + 8 * (j // 2) + 4 * (j % 2) + k
                plane[kind, k, j] = 96 * kind + 32 * k + j
    first = np.zeros((192, 256))
    second = np.zeros((256, 192))
    for a in range(2):
        for b in range(2):
            for k in range(3):
                first[np.ix_(plane[a, k], tile[b, k])] = step[a][b]
                second[np.ix_(tile[a, k], plane[b, k])] = step[a][b]
    return first.astype(np.float32), second.astype(np.float32)


def thirds(matrix):
    return jnp.stack(split3(jnp.asarray(matrix)))


def dot(a, b):
    return jnp.dot(a, b, preferred_element_type=f32)


def dot_nt(a, b):
    return lax.dot_general(a, b, (((1,), (1,)), ((), ())), preferred_element_type=f32)


def split2(x):
    high = x.astype(bf16)
    low = (x - high.astype(f32)).astype(bf16)
    return high, low


def split3(x):
    high = x.astype(bf16)
    rest = x - high.astype(f32)
    mid = rest.astype(bf16)
    low = (rest - mid.astype(f32)).astype(bf16)
    return high, mid, low


def parts3(x):
    high, mid, low = split3(x)
    return high.astype(f32), mid.astype(f32), low.astype(f32)


def moved_exactly(rows, hot, product):
    count = rows.shape[0]
    high, mid, low = split3(rows)
    out = product(jnp.concatenate([high, mid, low], axis=0), hot)
    return out[:count] + out[count : 2 * count] + out[2 * count :]


def by_thirds(matrix_ref, x):
    high, mid, low = split3(x)
    both = jnp.concatenate([high, mid], axis=1)
    out = dot(matrix_ref[0], both) + dot(matrix_ref[1], both)
    small = dot(matrix_ref[0], low) + dot(matrix_ref[2], high)
    return out[:, :SLOTS] + (out[:, SLOTS:] + small)


def rolled(x, shift):
    return pltpu.roll(x, shift, 1)


def bonds(planes, used_oxygen):
    one = [rolled(x, SLOTS - MOLS) for x in planes]
    two = [rolled(x, SLOTS - 2 * MOLS) for x in planes]
    d1 = [x - a for x, a in zip(planes, one)]
    d2 = [x - a for x, a in zip(planes, two)]
    d3 = [a - b for a, b in zip(one, two)]
    c1 = bond_stiffness * (d1[0] * d1[0] + d1[1] * d1[1] + d1[2] * d1[2] - bond_square)
    c2 = bond_stiffness * (d2[0] * d2[0] + d2[1] * d2[1] + d2[2] * d2[2] - bond_square)
    c3 = angle_stiffness * (d3[0] * d3[0] + d3[1] * d3[1] + d3[2] * d3[2] - angle_square)
    c1, c2, c3 = c1 * used_oxygen, c2 * used_oxygen, c3 * used_oxygen
    out = []
    for k in range(3):
        a, b, c = c1 * d1[k], c2 * d2[k], c3 * d3[k]
        out.append(rolled(a - c, MOLS) + rolled(b + c, 2 * MOLS) - (a + b))
    return out


def patterns():
    lane = lax.broadcasted_iota(jnp.int32, (1, SLOTS), 1)
    is_oxygen = jnp.where(lane < MOLS, 1.0, 0.0).astype(f32)
    charge = jnp.where(lane < MOLS, charge_oxygen, charge_hydrogen).astype(f32)
    return is_oxygen, charge


def bead_rows(bead):
    row = lax.broadcasted_iota(jnp.int32, (8, SLOTS), 0)
    return (row >= 4 * bead) & (row < 4 * bead + 3), row == 4 * bead + 3, row == (4 * bead + 4) % 8


def left_features(xyz, norm, rows):
    _, is_norm, is_one = rows
    full = jnp.where(is_norm, norm + coulomb_soft, jnp.where(is_one, 1.0, xyz))
    h, m, l = parts3(full)
    return jnp.concatenate([h, h, m, m, h, l], axis=0).astype(bf16)


def right_features(xyz, norm, rows):
    _, is_norm, is_one = rows
    full = jnp.where(is_norm, 1.0, jnp.where(is_one, norm, -2.0 * xyz))
    h, m, l = parts3(full)
    return jnp.concatenate([h, m, h, m, l, h], axis=0).astype(bf16)


def sum_features(xyz, rows, weight):
    full = jnp.where(rows[1], 1.0, xyz) * weight
    high = full.astype(bf16).astype(f32)
    return jnp.concatenate([high, full - high], axis=0).astype(bf16)


def squared(xyz):
    return jnp.sum(xyz * xyz, axis=0, keepdims=True)


def pulled(xyz, sums, bead):
    return xyz * sums[4 * bead + 3 : 4 * bead + 4, :] - sums


def folded(out):
    return out[0:8] + out[8:16]


CHUNK = 32


class Forces:
    def __init__(self, tile_of, used_of, own_ref, next_ref, mask_ref, lj_mask_ref, near_ref, ox_ref, feats_ref, ox_feats_ref):
        self.tile_of, self.used_of, self.own_ref, self.next_ref = tile_of, used_of, own_ref, next_ref
        self.mask_ref, self.lj_mask_ref, self.near_ref, self.ox_ref = mask_ref, lj_mask_ref, near_ref, ox_ref
        self.feats_ref, self.ox_feats_ref = feats_ref, ox_feats_ref
        self.is_oxygen, self.charge = patterns()
        self.rows = [bead_rows(bead) for bead in range(2)]
        self.row = lax.broadcasted_iota(jnp.int32, (8, SLOTS), 0)
        self.lane = lax.broadcasted_iota(jnp.int32, (8, SLOTS), 1)

    def xyz(self, c, bead, cell_shift):
        shift = jnp.where(self.row == 4 * bead, 0.5 - cell_shift, 0.5)
        return jnp.where(self.rows[bead][0], self.tile_of(c) - shift, 0.0)

    def squares(self, c, bead, alone=False):
        rows, lane = self.rows[bead], self.lane
        used, used2 = self.used_of(c), self.used_of(c + 1)
        xyz, xyz2 = self.xyz(c, bead, 0.0), self.xyz(c + 1, bead, 1.0)
        norm, norm2 = squared(xyz), squared(xyz2)
        left = left_features(xyz, norm, rows).T
        right2 = right_features(xyz2, norm2, rows)
        feats = sum_features(xyz, rows, used * self.charge)
        feats2 = sum_features(xyz2, rows, used2 * self.charge)
        self.feats_ref[bead] = jnp.concatenate([feats, feats2], axis=1)
        if alone:
            self.near_ref[bead, :, SLOTS:] = dot(left, right2)
            return
        right = jnp.concatenate([right_features(xyz, norm, rows), right2], axis=1)
        self.near_ref[bead] = dot(left, right)
        used0, xyz0 = self.used_of(c - 1), self.xyz(c - 1, bead, -1.0)
        three = jnp.where(
            lane < MOLS,
            xyz0,
            jnp.where(lane < 2 * MOLS, rolled(xyz, MOLS), rolled(xyz2, 2 * MOLS)),
        )
        ox = jnp.where(
            lane[:1] < MOLS,
            used0,
            jnp.where(
                lane[:1] < 2 * MOLS,
                rolled(used, MOLS),
                jnp.where(lane[:1] < 3 * MOLS, rolled(used2, 2 * MOLS), 0.0),
            ),
        )
        right = right_features(three, squared(three) + (lennard_soft - coulomb_soft), rows)
        self.ox_ref[bead] = dot(left[:48], right)
        self.ox_feats_ref[bead] = sum_features(three, rows, ox)

    def next_sums(self, c, bead, g):
        xyz2 = self.xyz(c + 1, bead, 1.0)
        feats = self.feats_ref[bead, :, :SLOTS]
        sums = folded(dot(feats, g[0]) + dot(feats, g[1]))
        return pulled(xyz2, sums, bead) * (coulomb_scale * self.used_of(c + 1) * self.charge)

    def sums(self, c, bead):
        high, low = [], []
        for i in range(0, SLOTS, CHUNK):
            part = self.near_ref[bead, i : i + CHUNK]
            part = jnp.concatenate([part[:, :SLOTS] + self.mask_ref[i : i + CHUNK], part[:, SLOTS:]], axis=1)
            y = lax.rsqrt(part)
            h, l = split2(y * y * y)
            high.append(h)
            low.append(l)
        high, low = jnp.concatenate(high, axis=0), jnp.concatenate(low, axis=0)
        y = lax.rsqrt(self.ox_ref[bead] + self.lj_mask_ref[...])
        inverse = y * y
        cubed = (inverse * inverse) * (inverse * sigma_square**3)
        g = cubed * (cubed * (48.0 * well_depth) - 24.0 * well_depth) * inverse
        ox_high, ox_low = split2(g)
        xyz = self.xyz(c, bead, 0.0)
        used = self.used_of(c)
        feats = self.feats_ref[bead]
        near = folded(dot_nt(feats, high) + dot_nt(feats, low))
        after = self.next_sums(c, bead, (high[:, SLOTS:], low[:, SLOTS:]))
        ox_feats = self.ox_feats_ref[bead]
        ox = folded(dot_nt(ox_feats, ox_high) + dot_nt(ox_feats, ox_low))
        ox = jnp.concatenate([ox, jnp.zeros((8, SLOTS - 48), f32)], axis=1)
        force = pulled(xyz, near, bead) * (coulomb_scale * used * self.charge)
        return force + pulled(xyz, ox, bead) * (used * self.is_oxygen), after

    def first_halo(self):
        out = []
        for bead in range(2):
            self.squares(0, bead, alone=True)
        for bead in range(2):
            y = lax.rsqrt(self.near_ref[bead, :, SLOTS:])
            out.append(self.next_sums(0, bead, split2(y * y * y)))
        self.next_ref[1] = jnp.where(self.row < 4, out[0], out[1])

    def cells(self, cell_of, count):
        for bead in range(2):
            self.squares(cell_of(0), bead)

        def body(i, carry):
            c = cell_of(i)
            follows = cell_of(jnp.minimum(i + 1, count - 1))
            near0, after0 = self.sums(c, 0)
            self.squares(follows, 0)
            near1, after1 = self.sums(c, 1)
            self.squares(follows, 1)
            self.own_ref[c] = jnp.where(self.row < 4, near0, near1)
            self.next_ref[c + 1] = jnp.where(self.row < 4, after0, after1)
            return carry

        lax.fori_loop(0, count, body, 0, unroll=2)


def kernel(
    pos_ref,
    mom_ref,
    ids_ref,
    first_ref,
    second_ref,
    x_out,
    p_out,
    raw,
    hot,
    tiles,
    moms,
    own_ref,
    next_ref,
    mask_ref,
    lj_mask_ref,
    near_ref,
    ox_ref,
    feats_ref,
    ox_feats_ref,
    sent_v,
    mode_in,
    mode_out,
    back_x,
    back_v,
    halo_send,
    halo_recv,
    in_send,
    in_recv,
    out_send,
    out_recv,
    v_recv,
):
    b = lax.axis_index("bead")
    s = lax.axis_index("space")
    far = lax.rem(s + FLIP, SPACE)
    right = lax.rem(s + 1, SPACE)
    left = lax.rem(s + SPACE - 1, SPACE)
    x_own, z_own = b // 4, lax.rem(b, 4)
    late = z_own >= 2
    z_far = z_own + jnp.where(s < SPACE // 2, 1, 2)

    def far_first(i):
        return lax.rem(x_own + 2 + lax.rem(i, 4), 4) * 4 + lax.rem(z_far + i // 4, 4)

    barrier = pltpu.get_barrier_semaphore()

    def hello(peer, carry):
        pl.semaphore_signal(barrier, inc=1, device_id=(peer, far), device_id_type=MESH)
        return carry

    lax.fori_loop(0, GROUP, hello, 0)
    for who in (left, right):
        pl.semaphore_signal(barrier, inc=1, device_id=(b, who), device_id_type=MESH)

    raw[...] = jnp.zeros_like(raw)
    for bead in range(2):
        for k in range(3):
            raw[pl.ds(4 * bead + k, CELLS, stride=16), :] = pos_ref[bead, k]
            raw[pl.ds(8 + 4 * bead + k, CELLS, stride=16), :] = mom_ref[bead, k]

    sub = lax.broadcasted_iota(jnp.int32, (SLOTS, SLOTS), 0)
    lane = lax.broadcasted_iota(jnp.int32, (SLOTS, SLOTS), 1)
    same = (sub % MOLS == lane % MOLS) & (sub < 3 * MOLS) & (lane < 3 * MOLS)
    mask_ref[...] = jnp.where(same, BIG, 0.0).astype(f32)
    lj_mask_ref[...] = jnp.where(lane[:48] == sub[:48] + MOLS, BIG, 0.0).astype(f32)

    ids = jnp.full((CELLS, SLOTS), SLOTS, jnp.int32)
    lane16 = lane[:CELLS]
    for t in range(3):
        padded = jnp.concatenate([ids_ref[t], jnp.zeros((CELLS, SLOTS - MOLS), jnp.int32)], axis=1)
        here = (lane16 >= t * MOLS) & (lane16 < (t + 1) * MOLS)
        ids = jnp.where(here, padded if t == 0 else rolled(padded, t * MOLS), ids)
    used_all = jnp.where(ids < SLOTS, 1.0, 0.0).astype(f32)
    above = jnp.where(sub < lane, 1.0, 0.0).astype(bf16)
    spare = dot((1.0 - used_all).astype(bf16), above)
    keys = jnp.where(ids < SLOTS, ids.astype(f32), spare + 1000.0)
    ones = jnp.ones((SLOTS, SLOTS), bf16)
    sub_f = sub.astype(f32)
    row16 = lax.broadcasted_iota(jnp.int32, (16, SLOTS), 0)

    def taken_below(c):
        key = keys[c : c + 1]
        return dot(jnp.where(key < sub_f, 1.0, jnp.where(key == sub_f, 0.5, 0.0)).astype(bf16), ones)

    ahead = [taken_below(c) for c in range(2)]
    for c in range(CELLS):
        if c + 2 < CELLS:
            ahead.append(taken_below(c + 2))
        key = keys[c : c + 1]
        spare_key = (sub_f + 1000.0) - ahead[c]
        place = jnp.where((sub_f == key) | (spare_key == key), 1.0, 0.0).astype(bf16)
        hot[c] = place
        rows = moved_exactly(raw[16 * c : 16 * c + 16], place, dot)
        rows = jnp.where(row16 == 3, used_all[c : c + 1], rows)
        tiles[c + 1] = rows[:8]
        moms[c] = rows[8:]

    def beside(first, last, below, above, at):
        return [
            pltpu.make_async_remote_copy(
                src_ref=first,
                dst_ref=above,
                send_sem=halo_send.at[at],
                recv_sem=halo_recv.at[at],
                device_id=(b, left),
                device_id_type=MESH,
            ),
            pltpu.make_async_remote_copy(
                src_ref=last,
                dst_ref=below,
                send_sem=halo_send.at[at + 1],
                recv_sem=halo_recv.at[at + 1],
                device_id=(b, right),
                device_id_type=MESH,
            ),
        ]

    def send_in(kind, ref, first):
        def send(i, carry):
            peer = far_first(i)
            pltpu.make_async_remote_copy(
                src_ref=ref.at[peer + first],
                dst_ref=mode_in.at[kind, b],
                send_sem=in_send.at[kind],
                recv_sem=in_recv.at[kind],
                device_id=(peer, far),
                device_id_type=MESH,
            ).start()
            return carry

        lax.fori_loop(0, GROUP, send, 0)

    halos = beside(tiles.at[1], tiles.at[CELLS], tiles.at[0], tiles.at[CELLS + 1], 0)

    def greet():
        pl.semaphore_wait(barrier, GROUP + 2)
        for copy in halos:
            copy.start()
        send_in(0, tiles, 1)

    is_oxygen, _ = patterns()
    used_planes = jnp.concatenate([used_all, used_all], axis=0)
    used_ox = used_planes * is_oxygen
    inverse_mass = 1.0 - (15.0 / 16.0) * used_ox
    mass = 1.0 + 15.0 * used_ox

    def used_of(c):
        return tiles[c, 3:4, :]

    tiles_rows = tiles.reshape((CELLS + 2) * 8, SLOTS)
    moms_rows = moms.reshape(CELLS * 8, SLOTS)
    own_rows = own_ref.reshape((CELLS + 2) * 8, SLOTS)
    next_rows = next_ref.reshape((CELLS + 2) * 8, SLOTS)
    sent_rows = sent_v.reshape(CELLS * 8, SLOTS)
    back_x_rows = back_x.reshape((CELLS + 2) * 8, SLOTS)
    back_v_rows = back_v.reshape(CELLS * 8, SLOTS)

    def plane(ref, start, k):
        return jnp.concatenate(
            [ref[pl.ds(start + 4 * bead + k, CELLS, stride=8), :] for bead in range(2)], axis=0
        )

    scratch = (own_ref, next_ref, mask_ref, lj_mask_ref, near_ref, ox_ref, feats_ref, ox_feats_ref)
    now = Forces(lambda c: tiles[c], used_of, *scratch)
    now.cells(lambda i: i + 2, 4)
    pl.when(late)(greet)
    now.cells(lambda i: i + 6, CELLS - 6)
    pl.when(jnp.logical_not(late))(greet)
    for copy in halos:
        copy.wait()
    now.cells(lambda i: CELLS - (CELLS - 1) * i, 2)
    now.first_halo()
    inner = bonds([plane(tiles_rows, 8, k) for k in range(3)], used_ox)
    sent_v[...] = jnp.zeros_like(sent_v)
    for k in range(3):
        outer = plane(own_rows, 8, k) + plane(next_rows, 8, k)
        p = plane(moms_rows, 0, k) + (0.5 * outer_step) * outer
        v = (p + (0.5 * inner_step) * inner[k]) * inverse_mass
        for bead in range(2):
            sent_rows[pl.ds(4 * bead + k, CELLS, stride=8), :] = v[CELLS * bead : CELLS * bead + CELLS]

    send_in(1, sent_v, 0)

    def all_of(kind, ref, send_sem, recv_sem):
        return pltpu.make_async_remote_copy(
            src_ref=ref,
            dst_ref=mode_in.at[kind],
            send_sem=send_sem,
            recv_sem=recv_sem,
            device_id=(b, far),
            device_id_type=MESH,
        )

    all_of(0, tiles.at[pl.ds(1, CELLS)], in_send.at[0], in_recv.at[0]).wait()
    all_of(1, sent_v, in_send.at[1], in_recv.at[1]).wait()

    mode_rows = mode_in[...].reshape(256, SLOTS)
    mode_ox = mode_in[0, 0, 3:4, :] * is_oxygen
    mode_inverse = 1.0 - (15.0 / 16.0) * mode_ox
    evolved = by_thirds(first_ref, mode_rows)
    pull = bonds([evolved[32 * k : 32 * k + 32] for k in range(3)], mode_ox)
    kicked = [evolved[96 + 32 * k : 128 + 32 * k] + (inner_step * mode_inverse) * pull[k] for k in range(3)]
    state = jnp.concatenate([evolved[:96], *kicked], axis=0)
    mode_out[...] = by_thirds(second_ref, state).reshape(2, GROUP, 8, SLOTS)

    def back(kind, dst, recv_sem):
        def send(i, carry):
            peer = far_first(i)
            pltpu.make_async_remote_copy(
                src_ref=mode_out.at[kind, peer],
                dst_ref=dst,
                send_sem=out_send.at[kind],
                recv_sem=recv_sem,
                device_id=(peer, far),
                device_id_type=MESH,
            ).start()
            return carry

        lax.fori_loop(0, GROUP, send, 0)

    back(0, back_x.at[b + 1], out_recv.at[b + 1])
    back(1, back_v.at[b], v_recv)

    def arrived(c):
        pltpu.make_async_copy(back_x.at[c], back_x.at[c], out_recv.at[c]).wait()

    halos = beside(back_x.at[1], back_x.at[CELLS], back_x.at[0], back_x.at[CELLS + 1], 2)
    for c, copy in ((1, halos[0]), (CELLS, halos[1])):
        arrived(c)
        copy.start()
    for c in range(2, CELLS):
        arrived(c)

    then = Forces(lambda c: back_x[c], used_of, *scratch)
    then.cells(lambda i: i + 2, CELLS - 2)
    for copy in halos:
        copy.wait()
    then.cells(lambda i: CELLS - (CELLS - 1) * i, 2)
    then.first_halo()
    inner = bonds([plane(back_x_rows, 8, k) for k in range(3)], used_ox)
    pltpu.make_async_copy(back_v, back_v, v_recv).wait()
    for k in range(3):
        outer = plane(own_rows, 8, k) + plane(next_rows, 8, k)
        p = mass * plane(back_v_rows, 0, k) + (0.5 * inner_step) * inner[k]
        p = p + (0.5 * outer_step) * outer
        x = plane(back_x_rows, 8, k)
        for bead in range(2):
            half = slice(CELLS * bead, CELLS * bead + CELLS)
            raw[pl.ds(4 * bead + k, CELLS, stride=16), :] = x[half]
            raw[pl.ds(8 + 4 * bead + k, CELLS, stride=16), :] = p[half]
    for c in range(CELLS):
        raw[16 * c : 16 * c + 16] = moved_exactly(raw[16 * c : 16 * c + 16], hot[c], dot_nt)
    for bead in range(2):
        for k in range(3):
            x_out[bead, k] = raw[pl.ds(4 * bead + k, CELLS, stride=16), :]
            p_out[bead, k] = raw[pl.ds(8 + 4 * bead + k, CELLS, stride=16), :]

    pltpu.make_async_copy(mode_out.at[0], mode_out.at[0], out_send.at[0]).wait()
    pltpu.make_async_copy(mode_out.at[1], mode_out.at[1], out_send.at[1]).wait()


def local(positions, momenta, molecules):
    ids = jnp.transpose(molecules, (2, 0, 1))
    first, second = propagators()
    vmem = pl.BlockSpec(memory_space=pltpu.VMEM)
    return pl.pallas_call(
        kernel,
        out_shape=[jax.ShapeDtypeStruct(positions.shape, f32)] * 2,
        in_specs=[vmem] * 5,
        out_specs=[vmem] * 2,
        scratch_shapes=[
            pltpu.VMEM((CELLS * 16, SLOTS), f32),
            pltpu.VMEM((CELLS, SLOTS, SLOTS), bf16),
            pltpu.VMEM((CELLS + 2, 8, SLOTS), f32),
            pltpu.VMEM((CELLS, 8, SLOTS), f32),
            pltpu.VMEM((CELLS + 2, 8, SLOTS), f32),
            pltpu.VMEM((CELLS + 2, 8, SLOTS), f32),
            pltpu.VMEM((SLOTS, SLOTS), f32),
            pltpu.VMEM((48, SLOTS), f32),
            pltpu.VMEM((2, SLOTS, 2 * SLOTS), f32),
            pltpu.VMEM((2, 48, SLOTS), f32),
            pltpu.VMEM((2, 16, 2 * SLOTS), bf16),
            pltpu.VMEM((2, 16, SLOTS), bf16),
            pltpu.VMEM((CELLS, 8, SLOTS), f32),
            pltpu.VMEM((2, GROUP, 8, SLOTS), f32),
            pltpu.VMEM((2, GROUP, 8, SLOTS), f32),
            pltpu.VMEM((CELLS + 2, 8, SLOTS), f32),
            pltpu.VMEM((CELLS, 8, SLOTS), f32),
            pltpu.SemaphoreType.DMA((4,)),
            pltpu.SemaphoreType.DMA((4,)),
            pltpu.SemaphoreType.DMA((2,)),
            pltpu.SemaphoreType.DMA((2,)),
            pltpu.SemaphoreType.DMA((2,)),
            pltpu.SemaphoreType.DMA((CELLS + 2,)),
            pltpu.SemaphoreType.DMA,
        ],
        compiler_params=pltpu.CompilerParams(collective_id=0, has_side_effects=True),
    )(positions, momenta, ids, thirds(first), thirds(second))


def solution(mesh):
    wide = P("bead", None, "space", None)
    return jax.shard_map(
        local,
        mesh=mesh,
        in_specs=(wide, wide, P("space", None, None)),
        out_specs=(wide, wide),
        check_vma=False,
    )
```

```python
import functools

import jax
import jax.numpy as jnp
import numpy as np
from jax import lax
from jax.experimental import pallas as pl
from jax.experimental.pallas import tpu as pltpu
from jax.sharding import PartitionSpec as P

MESH = pl.DeviceIdType.MESH

SLOTS = 128
MOLS = 42
CELLS = 16
BEADS = 32
GROUP = 16
SPACE = 32
KEEPERS = ((0, 3, 1, 2), (0, 0, 1, 1))
GREET_MID = (0, 1)
ROWS = (7, 6)
FLIP = 16

charge_oxygen = -0.8476
charge_hydrogen = 0.4238
coulomb_scale = 24.0
coulomb_soft = 0.004
well_depth = 0.02
sigma_square = 0.0841
lennard_soft = 0.04
bond_stiffness = 20000.0
bond_square = 0.0081
angle_stiffness = 5000.0
angle_square = 0.0204
cycle_frequency = 60.0
outer_step = 0.02
inner_step = 0.01
BIG = 2.0**100

f32 = jnp.float32
bf16 = jnp.bfloat16


def propagators():
    ids = np.arange(BEADS)
    angles = 2.0 * np.pi / BEADS * (ids[:, None] * ids[None, :] % BEADS)
    half = BEADS // 2
    col = ids[None, :]
    transform = np.where(
        col == 0,
        np.sqrt(1.0 / BEADS),
        np.where(
            col < half,
            np.sqrt(2.0 / BEADS) * np.cos(angles),
            np.where(
                col == half,
                np.sqrt(1.0 / BEADS) * np.cos(angles),
                np.sqrt(2.0 / BEADS) * np.sin(angles),
            ),
        ),
    )
    freq = 2.0 * cycle_frequency * np.sin(np.pi * ids / BEADS)
    cosk = np.cos(freq * inner_step)
    springk = freq * np.sin(freq * inner_step)
    driftk = np.where(ids == 0, inner_step, np.sin(freq * inner_step) / np.where(ids == 0, 1.0, freq))
    on = [transform @ np.diag(v) @ transform.T for v in (cosk, driftk, -springk)]
    step = [[on[0], on[1]], [on[2], on[0]]]
    tile = np.zeros((2, 3, BEADS), int)
    plane = np.zeros((2, 3, BEADS), int)
    for kind in range(2):
        for k in range(3):
            for j in range(BEADS):
                tile[kind, k, j] = 128 * kind + 8 * (j // 2) + 3 * (j % 2) + k
                plane[kind, k, j] = 96 * kind + 32 * k + j
    first = np.zeros((192, 256))
    second = np.zeros((256, 192))
    for a in range(2):
        for b in range(2):
            for k in range(3):
                first[np.ix_(plane[a, k], tile[b, k])] = step[a][b]
                second[np.ix_(tile[a, k], plane[b, k])] = step[a][b]
    return first.astype(np.float32), second.astype(np.float32)


def thirds(matrix):
    return jnp.stack(split3(jnp.asarray(matrix)))


def dot(a, b):
    return jnp.dot(a, b, preferred_element_type=f32)


def dot_nt(a, b):
    return lax.dot_general(a, b, (((1,), (1,)), ((), ())), preferred_element_type=f32)


def split2(x):
    high = x.astype(bf16)
    low = (x - high.astype(f32)).astype(bf16)
    return high, low


def split3(x):
    high = x.astype(bf16)
    rest = x - high.astype(f32)
    mid = rest.astype(bf16)
    low = (rest - mid.astype(f32)).astype(bf16)
    return high, mid, low


def parts3(x):
    high, mid, low = split3(x)
    return high.astype(f32), mid.astype(f32), low.astype(f32)


def moved_exactly(rows, hot, product):
    count = rows.shape[0]
    high, mid, low = split3(rows)
    out = product(jnp.concatenate([high, mid, low], axis=0), hot)
    return out[:count] + out[count : 2 * count] + out[2 * count :]


def by_thirds(matrix_ref, x):
    high, mid, low = split3(x)
    both = jnp.concatenate([high, mid], axis=1)
    out = dot(matrix_ref[0], both) + dot(matrix_ref[1], both)
    small = dot(matrix_ref[0], low) + dot(matrix_ref[2], high)
    return out[:, : x.shape[1]] + (out[:, x.shape[1] :] + small)


def rolled(x, shift):
    return pltpu.roll(x, shift, 1)


def bonds(planes, used_oxygen):
    one = [rolled(x, SLOTS - MOLS) for x in planes]
    two = [rolled(x, SLOTS - 2 * MOLS) for x in planes]
    d1 = [x - a for x, a in zip(planes, one)]
    d2 = [x - a for x, a in zip(planes, two)]
    d3 = [a - b for a, b in zip(one, two)]
    c1 = bond_stiffness * (d1[0] * d1[0] + d1[1] * d1[1] + d1[2] * d1[2] - bond_square)
    c2 = bond_stiffness * (d2[0] * d2[0] + d2[1] * d2[1] + d2[2] * d2[2] - bond_square)
    c3 = angle_stiffness * (d3[0] * d3[0] + d3[1] * d3[1] + d3[2] * d3[2] - angle_square)
    c1, c2, c3 = c1 * used_oxygen, c2 * used_oxygen, c3 * used_oxygen
    out = []
    for k in range(3):
        a, b, c = c1 * d1[k], c2 * d2[k], c3 * d3[k]
        out.append(rolled(a - c, MOLS) + rolled(b + c, 2 * MOLS) - (a + b))
    return out


def patterns():
    lane = lax.broadcasted_iota(jnp.int32, (1, SLOTS), 1)
    is_oxygen = jnp.where(lane < MOLS, 1.0, 0.0).astype(f32)
    charge = jnp.where(lane < MOLS, charge_oxygen, charge_hydrogen).astype(f32)
    return is_oxygen, charge


def bead_rows(bead):
    row = lax.broadcasted_iota(jnp.int32, (8, SLOTS), 0)
    return (row >= 3 * bead) & (row < 3 * bead + 3), row == 6, row == 7


def left_features(xyz, norm, rows):
    _, is_norm, is_one = rows
    full = jnp.where(is_norm, norm + coulomb_soft, jnp.where(is_one, 1.0, xyz))
    h, m, l = parts3(full)
    return jnp.concatenate([h, h, m, m, h, l], axis=0).astype(bf16)


def right_features(xyz, norm, rows):
    _, is_norm, is_one = rows
    full = jnp.where(is_norm, 1.0, jnp.where(is_one, norm, -2.0 * xyz))
    h, m, l = parts3(full)
    return jnp.concatenate([h, m, h, m, l, h], axis=0).astype(bf16)


def sum_features(xyz, rows, weight):
    full = jnp.where(rows[1], 1.0, xyz) * weight
    high = full.astype(bf16).astype(f32)
    return jnp.concatenate([high, full - high], axis=0).astype(bf16)


def squared(xyz):
    return jnp.sum(xyz * xyz, axis=0, keepdims=True)


def pulled(xyz, sums, bead):
    return xyz * sums[6:7, :] - sums


def folded(out):
    return out[0:8] + out[8:16]


CHUNK = 32


class Forces:
    def __init__(self, tile_of, used_of, own_ref, next_ref, mask_ref, lj_mask_ref, near_ref, ox_ref, feats_ref, ox_feats_ref):
        self.tile_of, self.used_of, self.own_ref, self.next_ref = tile_of, used_of, own_ref, next_ref
        self.mask_ref, self.lj_mask_ref, self.near_ref, self.ox_ref = mask_ref, lj_mask_ref, near_ref, ox_ref
        self.feats_ref, self.ox_feats_ref = feats_ref, ox_feats_ref
        self.is_oxygen, self.charge = patterns()
        self.rows = [bead_rows(bead) for bead in range(2)]
        self.row = lax.broadcasted_iota(jnp.int32, (8, SLOTS), 0)
        self.lane = lax.broadcasted_iota(jnp.int32, (8, SLOTS), 1)

    def xyz(self, c, bead, cell_shift):
        shift = jnp.where(self.row == 3 * bead, 0.5 - cell_shift, 0.5)
        return jnp.where(self.rows[bead][0], self.tile_of(c) - shift, 0.0)

    def squares(self, c, bead, alone=False):
        rows, lane = self.rows[bead], self.lane
        used, used2 = self.used_of(c), self.used_of(c + 1)
        xyz, xyz2 = self.xyz(c, bead, 0.0), self.xyz(c + 1, bead, 1.0)
        norm, norm2 = squared(xyz), squared(xyz2)
        left = left_features(xyz, norm, rows).T
        right2 = right_features(xyz2, norm2, rows)
        feats = sum_features(xyz, rows, used * self.charge)
        feats2 = sum_features(xyz2, rows, used2 * self.charge)
        self.feats_ref[bead] = jnp.concatenate([feats, feats2], axis=1)
        if alone:
            self.near_ref[bead, :, SLOTS:] = dot(left, right2)
            return
        right = jnp.concatenate([right_features(xyz, norm, rows), right2], axis=1)
        self.near_ref[bead] = dot(left, right)
        used0, xyz0 = self.used_of(c - 1), self.xyz(c - 1, bead, -1.0)
        three = jnp.where(
            lane < MOLS,
            xyz0,
            jnp.where(lane < 2 * MOLS, rolled(xyz, MOLS), rolled(xyz2, 2 * MOLS)),
        )
        ox = jnp.where(
            lane[:1] < MOLS,
            used0,
            jnp.where(
                lane[:1] < 2 * MOLS,
                rolled(used, MOLS),
                jnp.where(lane[:1] < 3 * MOLS, rolled(used2, 2 * MOLS), 0.0),
            ),
        )
        right = right_features(three, squared(three) + (lennard_soft - coulomb_soft), rows)
        self.ox_ref[bead] = dot(left[:48], right)
        self.ox_feats_ref[bead] = sum_features(three, rows, ox)

    def next_sums(self, c, bead, g):
        xyz2 = self.xyz(c + 1, bead, 1.0)
        feats = self.feats_ref[bead, :, :SLOTS]
        sums = folded(dot(feats, g[0]) + dot(feats, g[1]))
        return pulled(xyz2, sums, bead) * (coulomb_scale * self.used_of(c + 1) * self.charge)

    def sums(self, c, bead):
        high, low = [], []
        for i in range(0, SLOTS, CHUNK):
            part = self.near_ref[bead, i : i + CHUNK]
            part = jnp.concatenate([part[:, :SLOTS] + self.mask_ref[i : i + CHUNK], part[:, SLOTS:]], axis=1)
            y = lax.rsqrt(part)
            h, l = split2(y * y * y)
            high.append(h)
            low.append(l)
        high, low = jnp.concatenate(high, axis=0), jnp.concatenate(low, axis=0)
        y = lax.rsqrt(self.ox_ref[bead] + self.lj_mask_ref[...])
        inverse = y * y
        cubed = (inverse * inverse) * (inverse * sigma_square**3)
        g = cubed * (cubed * (48.0 * well_depth) - 24.0 * well_depth) * inverse
        ox_high, ox_low = split2(g)
        xyz = self.xyz(c, bead, 0.0)
        used = self.used_of(c)
        feats = self.feats_ref[bead]
        near = folded(dot_nt(feats, high) + dot_nt(feats, low))
        after = self.next_sums(c, bead, (high[:, SLOTS:], low[:, SLOTS:]))
        ox_feats = self.ox_feats_ref[bead]
        ox = folded(dot_nt(ox_feats, ox_high) + dot_nt(ox_feats, ox_low))
        ox = jnp.concatenate([ox, jnp.zeros((8, SLOTS - 48), f32)], axis=1)
        force = pulled(xyz, near, bead) * (coulomb_scale * used * self.charge)
        return force + pulled(xyz, ox, bead) * (used * self.is_oxygen), after

    def first_halo(self):
        out = []
        for bead in range(2):
            self.squares(0, bead, alone=True)
        for bead in range(2):
            y = lax.rsqrt(self.near_ref[bead, :, SLOTS:])
            out.append(self.next_sums(0, bead, split2(y * y * y)))
        self.next_ref[1] = jnp.where(self.row < 3, out[0], out[1])

    def cells(self, cell_of, count):
        for bead in range(2):
            self.squares(cell_of(0), bead)

        def body(i, carry):
            c = cell_of(i)
            follows = cell_of(jnp.minimum(i + 1, count - 1))
            near0, after0 = self.sums(c, 0)
            self.squares(follows, 0)
            near1, after1 = self.sums(c, 1)
            self.squares(follows, 1)
            self.own_ref[c] = jnp.where(self.row < 3, near0, near1)
            self.next_ref[c + 1] = jnp.where(self.row < 3, after0, after1)
            return carry

        lax.fori_loop(0, count, body, 0, unroll=2)


def evolve(first_ref, second_ref, mode_in, mode_out, back_x, back_v, in_recv, out_send, out_recv, v_recv, cells, slots, group):
    b = lax.axis_index("bead")
    is_oxygen, _ = patterns()
    for kind in range(2):
        received = mode_in.at[kind, pl.ds(0, slots), :, pl.ds(0, ROWS[kind])]
        pltpu.make_async_copy(received, received, in_recv.at[kind]).wait()
    rows = [mode_in[:, slot].reshape(256, SLOTS) for slot in range(slots)]
    evolved = by_thirds(first_ref, jnp.concatenate(rows, axis=1))
    states = []
    for slot in range(slots):
        oxygens = mode_in[0, slot, 0, 6:7, :] * is_oxygen
        inverse = 1.0 - (15.0 / 16.0) * oxygens
        mine = evolved[:, SLOTS * slot : SLOTS * slot + SLOTS]
        pull = bonds([mine[32 * k : 32 * k + 32] for k in range(3)], oxygens)
        kicked = [mine[96 + 32 * k : 128 + 32 * k] + (inner_step * inverse) * pull[k] for k in range(3)]
        states.append(jnp.concatenate([mine[:96], *kicked], axis=0))
    out = by_thirds(second_ref, jnp.concatenate(states, axis=1))
    for slot in range(slots):
        mode_out[:, slot] = out[:, SLOTS * slot : SLOTS * slot + SLOTS].reshape(2, GROUP, 8, SLOTS)

    def back(kind, slot, dst, recv_sem):
        def send(i, carry):
            peer = lax.rem(b // 4 + i, 4) * 4 + i // 4
            pltpu.make_async_remote_copy(
                src_ref=mode_out.at[kind, slot, peer, pl.ds(0, 6)],
                dst_ref=dst.at[pl.ds(0, 6)],
                send_sem=out_send.at[kind],
                recv_sem=recv_sem,
                device_id=(peer, group),
                device_id_type=MESH,
            ).start()
            return carry

        lax.fori_loop(0, GROUP, send, 0)

    for slot in range(slots):
        at = cells[slot]
        back(0, slot, back_x.at[at + 1], out_recv.at[at + 1])
    for slot in range(slots):
        back(1, slot, back_v.at[cells[slot]], v_recv)


def pick(group, two):
    return jnp.where(group < SPACE // 2, two[0], two[1]) != 0


def slots_of(row):
    return [row[:q].count(row[q]) for q in range(4)]


def table(group, of, at):
    rows = [list(of(row)) for row in KEEPERS]
    out = 0
    for i in range(4):
        value = rows[0][i] if rows[0][i] == rows[1][i] else jnp.where(group < SPACE // 2, rows[0][i], rows[1][i])
        out = value if i == 0 else jnp.where(at == i, value, out)
    return out


def kernel(
    pos_hbm,
    mom_hbm,
    ids_hbm,
    first_hbm,
    second_hbm,
    out,
    pos_ref,
    mom_ref,
    ids_ref,
    first_ref,
    second_ref,
    load_sem,
    raw,
    hot,
    tiles,
    moms,
    own_ref,
    next_ref,
    mask_ref,
    lj_mask_ref,
    near_ref,
    ox_ref,
    feats_ref,
    ox_feats_ref,
    sent_v,
    mode_in,
    mode_out,
    back_x,
    back_v,
    halo_send,
    halo_recv,
    in_send,
    in_recv,
    out_send,
    out_recv,
    v_recv,
):
    b = lax.axis_index("bead")
    s = lax.axis_index("space")
    far = lax.rem(s + FLIP, SPACE)
    right = lax.rem(s + 1, SPACE)
    left = lax.rem(s + SPACE - 1, SPACE)
    x_own, z_own = b // 4, lax.rem(b, 4)
    late = (z_own >= 2) | ((z_own == 1) & pick(s, GREET_MID))

    from_cell = jnp.where(z_own == 0, 8, 0)

    def keeper(j):
        return lax.rem(j, 4) * 4 + table(s, lambda row: row, j // 4)

    def slot_of(j):
        return table(s, slots_of, j // 4)

    kept = table(far, lambda row: [row.count(z) for z in range(4)], z_own)
    kept_cells = [
        x_own + 4 * table(far, lambda row: [([q for q in range(4) if row[q] == z] + [0, 0])[k] for z in range(4)], z_own)
        for k in range(2)
    ]
    senders = table(s, lambda row: [4 * len(set(row))] * 4, 0)

    loads = [
        pltpu.make_async_copy(src, dst, load_sem.at[i])
        for i, (src, dst) in enumerate(
            ((pos_hbm, pos_ref), (mom_hbm, mom_ref), (ids_hbm, ids_ref), (first_hbm, first_ref), (second_hbm, second_ref))
        )
    ]
    for load in loads:
        load.start()

    barrier = pltpu.get_barrier_semaphore()

    def hello(peer, carry):
        pl.semaphore_signal(barrier, inc=1, device_id=(peer, far), device_id_type=MESH)
        return carry

    mode_in[...] = jnp.zeros_like(mode_in)

    @pl.when(kept > 0)
    def _():
        lax.fori_loop(0, GROUP, hello, 0)

    for who in (left, right):
        pl.semaphore_signal(barrier, inc=1, device_id=(b, who), device_id_type=MESH)

    for load in loads[:3]:
        load.wait()

    raw[...] = jnp.zeros_like(raw)
    for bead in range(2):
        for k in range(3):
            raw[pl.ds(3 * bead + k, CELLS, stride=16), :] = pos_ref[bead, k]
            raw[pl.ds(8 + 3 * bead + k, CELLS, stride=16), :] = mom_ref[bead, k]

    sub = lax.broadcasted_iota(jnp.int32, (SLOTS, SLOTS), 0)
    lane = lax.broadcasted_iota(jnp.int32, (SLOTS, SLOTS), 1)
    same = (sub % MOLS == lane % MOLS) & (sub < 3 * MOLS) & (lane < 3 * MOLS)
    mask_ref[...] = jnp.where(same, BIG, 0.0).astype(f32)
    lj_mask_ref[...] = jnp.where(lane[:48] == sub[:48] + MOLS, BIG, 0.0).astype(f32)

    ids = jnp.full((CELLS, SLOTS), SLOTS, jnp.int32)
    lane16 = lane[:CELLS]
    for t in range(3):
        padded = jnp.concatenate([ids_ref[t], jnp.zeros((CELLS, SLOTS - MOLS), jnp.int32)], axis=1)
        here = (lane16 >= t * MOLS) & (lane16 < (t + 1) * MOLS)
        ids = jnp.where(here, padded if t == 0 else rolled(padded, t * MOLS), ids)
    used_all = jnp.where(ids < SLOTS, 1.0, 0.0).astype(f32)
    above = jnp.where(sub < lane, 1.0, 0.0).astype(bf16)
    spare = dot((1.0 - used_all).astype(bf16), above)
    keys = jnp.where(ids < SLOTS, ids.astype(f32), spare + 1000.0)
    ones = jnp.ones((SLOTS, SLOTS), bf16)
    sub_f = sub.astype(f32)
    row16 = lax.broadcasted_iota(jnp.int32, (16, SLOTS), 0)

    def taken_below(c):
        key = keys[c : c + 1]
        return dot(jnp.where(key < sub_f, 1.0, jnp.where(key == sub_f, 0.5, 0.0)).astype(bf16), ones)

    ahead = [taken_below(c) for c in range(2)]
    for c in range(CELLS):
        if c + 2 < CELLS:
            ahead.append(taken_below(c + 2))
        key = keys[c : c + 1]
        spare_key = (sub_f + 1000.0) - ahead[c]
        place = jnp.where((sub_f == key) | (spare_key == key), 1.0, 0.0).astype(bf16)
        hot[c] = place
        rows = moved_exactly(raw[16 * c : 16 * c + 16], place, dot)
        rows = jnp.where(row16 == 6, used_all[c : c + 1], rows)
        tiles[c + 1] = rows[:8]
        moms[c] = rows[8:]

    def beside(ref, rows, at):
        return [
            pltpu.make_async_remote_copy(
                src_ref=ref.at[1, pl.ds(0, rows)],
                dst_ref=ref.at[CELLS + 1, pl.ds(0, rows)],
                send_sem=halo_send.at[at],
                recv_sem=halo_recv.at[at],
                device_id=(b, left),
                device_id_type=MESH,
            ),
            pltpu.make_async_remote_copy(
                src_ref=ref.at[CELLS, pl.ds(0, rows)],
                dst_ref=ref.at[0, pl.ds(0, rows)],
                send_sem=halo_send.at[at + 1],
                recv_sem=halo_recv.at[at + 1],
                device_id=(b, right),
                device_id_type=MESH,
            ),
        ]

    def send_in(kind, ref, first):
        def send(i, carry):
            j = lax.rem(from_cell + i, CELLS)
            pltpu.make_async_remote_copy(
                src_ref=ref.at[j + first, pl.ds(0, ROWS[kind])],
                dst_ref=mode_in.at[kind, slot_of(j), b, pl.ds(0, ROWS[kind])],
                send_sem=in_send.at[kind],
                recv_sem=in_recv.at[kind],
                device_id=(keeper(j), far),
                device_id_type=MESH,
            ).start()
            return carry

        lax.fori_loop(0, GROUP, send, 0)

    halos = beside(tiles, 7, 0)

    def greet():
        pl.semaphore_wait(barrier, senders + 2)
        for copy in halos:
            copy.start()

    is_oxygen, _ = patterns()
    used_planes = jnp.concatenate([used_all, used_all], axis=0)
    used_ox = used_planes * is_oxygen
    inverse_mass = 1.0 - (15.0 / 16.0) * used_ox
    mass = 1.0 + 15.0 * used_ox

    def used_of(c):
        return tiles[c, 6:7, :]

    tiles_rows = tiles.reshape((CELLS + 2) * 8, SLOTS)
    moms_rows = moms.reshape(CELLS * 8, SLOTS)
    own_rows = own_ref.reshape((CELLS + 2) * 8, SLOTS)
    next_rows = next_ref.reshape((CELLS + 2) * 8, SLOTS)
    sent_rows = sent_v.reshape(CELLS * 8, SLOTS)
    back_x_rows = back_x.reshape((CELLS + 2) * 8, SLOTS)
    back_v_rows = back_v.reshape(CELLS * 8, SLOTS)

    def plane(ref, start, k):
        return jnp.concatenate(
            [ref[pl.ds(start + 3 * bead + k, CELLS, stride=8), :] for bead in range(2)], axis=0
        )

    scratch = (own_ref, next_ref, mask_ref, lj_mask_ref, near_ref, ox_ref, feats_ref, ox_feats_ref)
    now = Forces(lambda c: tiles[c], used_of, *scratch)
    now.cells(lambda i: i + 2, 4)
    @pl.when(late)
    def _():
        greet()
        send_in(0, tiles, 1)

    now.cells(lambda i: i + 6, CELLS - 6)
    pl.when(jnp.logical_not(late))(greet)
    for copy in halos:
        copy.wait()

    @pl.when(jnp.logical_not(late))
    def _():
        send_in(0, tiles, 1)

    now.cells(lambda i: CELLS - (CELLS - 1) * i, 2)
    now.first_halo()
    inner = bonds([plane(tiles_rows, 8, k) for k in range(3)], used_ox)
    sent_v[...] = jnp.zeros_like(sent_v)
    for k in range(3):
        outer = plane(own_rows, 8, k) + plane(next_rows, 8, k)
        p = plane(moms_rows, 0, k) + (0.5 * outer_step) * outer
        v = (p + (0.5 * inner_step) * inner[k]) * inverse_mass
        for bead in range(2):
            sent_rows[pl.ds(3 * bead + k, CELLS, stride=8), :] = v[CELLS * bead : CELLS * bead + CELLS]

    send_in(1, sent_v, 0)

    evolution = (first_ref, second_ref, mode_in, mode_out, back_x, back_v, in_recv, out_send, out_recv, v_recv)

    for load in loads[3:]:
        load.wait()

    for count in range(1, 3):

        @pl.when(kept == count)
        def _():
            evolve(*evolution, kept_cells, count, far)

    def arrived(c):
        tile = back_x.at[c, pl.ds(0, 6)]
        pltpu.make_async_copy(tile, tile, out_recv.at[c]).wait()

    halos = beside(back_x, 6, 2)
    arrived(1)
    halos[0].start()
    for c in range(2, 9):
        arrived(c)
    then = Forces(lambda c: back_x[c], used_of, *scratch)
    then.cells(lambda i: i + 2, 6)
    for c in range(CELLS, 8, -1):
        arrived(c)
        if c == CELLS:
            halos[1].start()
    then.cells(lambda i: i + 8, 8)
    for copy in halos:
        copy.wait()
    then.cells(lambda i: CELLS - (CELLS - 1) * i, 2)
    then.first_halo()
    inner = bonds([plane(back_x_rows, 8, k) for k in range(3)], used_ox)
    received = back_v.at[:, pl.ds(0, 6)]
    pltpu.make_async_copy(received, received, v_recv).wait()
    for k in range(3):
        outer = plane(own_rows, 8, k) + plane(next_rows, 8, k)
        p = mass * plane(back_v_rows, 0, k) + (0.5 * inner_step) * inner[k]
        p = p + (0.5 * outer_step) * outer
        x = plane(back_x_rows, 8, k)
        for bead in range(2):
            half = slice(CELLS * bead, CELLS * bead + CELLS)
            raw[pl.ds(3 * bead + k, CELLS, stride=16), :] = x[half]
            raw[pl.ds(8 + 3 * bead + k, CELLS, stride=16), :] = p[half]
    for c in range(CELLS):
        raw[16 * c : 16 * c + 16] = moved_exactly(raw[16 * c : 16 * c + 16], hot[c], dot_nt)
    for bead in range(2):
        for k in range(3):
            out[0, bead, k] = raw[pl.ds(3 * bead + k, CELLS, stride=16), :]
            out[1, bead, k] = raw[pl.ds(8 + 3 * bead + k, CELLS, stride=16), :]

    for kind in range(2):
        sent = sent_v.at[:, pl.ds(0, ROWS[kind])]
        pltpu.make_async_copy(sent, sent, in_send.at[kind]).wait()

    def all_back(slots):
        for kind in range(2):
            sent = mode_out.at[kind, pl.ds(0, slots), :, pl.ds(0, 6)]
            pltpu.make_async_copy(sent, sent, out_send.at[kind]).wait()

    for count in range(1, 3):
        pl.when(kept == count)(functools.partial(all_back, count))


def local(positions, momenta, molecules):
    ids = jnp.transpose(molecules, (2, 0, 1))
    first, second = propagators()
    vmem = pl.BlockSpec(memory_space=pltpu.VMEM)
    both = pl.pallas_call(
        kernel,
        out_shape=jax.ShapeDtypeStruct((2, *positions.shape), f32),
        in_specs=[pl.BlockSpec(memory_space=pl.ANY)] * 5,
        out_specs=vmem,
        scratch_shapes=[
            pltpu.VMEM(positions.shape, f32),
            pltpu.VMEM(momenta.shape, f32),
            pltpu.VMEM(ids.shape, jnp.int32),
            pltpu.VMEM((3, 192, 256), bf16),
            pltpu.VMEM((3, 256, 192), bf16),
            pltpu.SemaphoreType.DMA((5,)),
            pltpu.VMEM((CELLS * 16, SLOTS), f32),
            pltpu.VMEM((CELLS, SLOTS, SLOTS), bf16),
            pltpu.VMEM((CELLS + 2, 8, SLOTS), f32),
            pltpu.VMEM((CELLS, 8, SLOTS), f32),
            pltpu.VMEM((CELLS + 2, 8, SLOTS), f32),
            pltpu.VMEM((CELLS + 2, 8, SLOTS), f32),
            pltpu.VMEM((SLOTS, SLOTS), f32),
            pltpu.VMEM((48, SLOTS), f32),
            pltpu.VMEM((2, SLOTS, 2 * SLOTS), f32),
            pltpu.VMEM((2, 48, SLOTS), f32),
            pltpu.VMEM((2, 16, 2 * SLOTS), bf16),
            pltpu.VMEM((2, 16, SLOTS), bf16),
            pltpu.VMEM((CELLS, 8, SLOTS), f32),
            pltpu.VMEM((2, 2, GROUP, 8, SLOTS), f32),
            pltpu.VMEM((2, 2, GROUP, 8, SLOTS), f32),
            pltpu.VMEM((CELLS + 2, 8, SLOTS), f32),
            pltpu.VMEM((CELLS, 8, SLOTS), f32),
            pltpu.SemaphoreType.DMA((4,)),
            pltpu.SemaphoreType.DMA((4,)),
            pltpu.SemaphoreType.DMA((2,)),
            pltpu.SemaphoreType.DMA((2,)),
            pltpu.SemaphoreType.DMA((2,)),
            pltpu.SemaphoreType.DMA((CELLS + 2,)),
            pltpu.SemaphoreType.DMA,
        ],
        compiler_params=pltpu.CompilerParams(collective_id=0, has_side_effects=True),
    )(positions, momenta, ids, thirds(first), thirds(second))
    return both[0], both[1]


def solution(mesh):
    wide = P("bead", None, "space", None)
    return jax.shard_map(
        local,
        mesh=mesh,
        in_specs=(wide, wide, P("space", None, None)),
        out_specs=(wide, wide),
        check_vma=False,
    )
```

```python
import functools

import jax
import jax.numpy as jnp
import numpy as np
from jax import lax
from jax.experimental import pallas as pl
from jax.experimental.pallas import tpu as pltpu
from jax.sharding import PartitionSpec as P

MESH = pl.DeviceIdType.MESH

SLOTS = 128
MOLS = 42
CELLS = 16
BEADS = 32
GROUP = 16
SPACE = 32
KEEPERS = ((0, 3, 1, 2), (0, 1, 1, 3))
GREET_MID = (0, 1)
ROWS = (7, 6)
FLIP = 16

charge_oxygen = -0.8476
charge_hydrogen = 0.4238
coulomb_scale = 24.0
coulomb_soft = 0.004
well_depth = 0.02
sigma_square = 0.0841
lennard_soft = 0.04
bond_stiffness = 20000.0
bond_square = 0.0081
angle_stiffness = 5000.0
angle_square = 0.0204
cycle_frequency = 60.0
outer_step = 0.02
inner_step = 0.01
BIG = 2.0**100

f32 = jnp.float32
bf16 = jnp.bfloat16


def propagators():
    ids = np.arange(BEADS)
    angles = 2.0 * np.pi / BEADS * (ids[:, None] * ids[None, :] % BEADS)
    half = BEADS // 2
    col = ids[None, :]
    transform = np.where(
        col == 0,
        np.sqrt(1.0 / BEADS),
        np.where(
            col < half,
            np.sqrt(2.0 / BEADS) * np.cos(angles),
            np.where(
                col == half,
                np.sqrt(1.0 / BEADS) * np.cos(angles),
                np.sqrt(2.0 / BEADS) * np.sin(angles),
            ),
        ),
    )
    freq = 2.0 * cycle_frequency * np.sin(np.pi * ids / BEADS)
    cosk = np.cos(freq * inner_step)
    springk = freq * np.sin(freq * inner_step)
    driftk = np.where(ids == 0, inner_step, np.sin(freq * inner_step) / np.where(ids == 0, 1.0, freq))
    on = [transform @ np.diag(v) @ transform.T for v in (cosk, driftk, -springk)]
    step = [[on[0], on[1]], [on[2], on[0]]]
    tile = np.zeros((2, 3, BEADS), int)
    plane = np.zeros((2, 3, BEADS), int)
    for kind in range(2):
        for k in range(3):
            for j in range(BEADS):
                tile[kind, k, j] = 128 * kind + 8 * (j // 2) + 3 * (j % 2) + k
                plane[kind, k, j] = 96 * kind + 32 * k + j
    first = np.zeros((192, 256))
    second = np.zeros((256, 192))
    for a in range(2):
        for b in range(2):
            for k in range(3):
                first[np.ix_(plane[a, k], tile[b, k])] = step[a][b]
                second[np.ix_(tile[a, k], plane[b, k])] = step[a][b]
    return first.astype(np.float32), second.astype(np.float32)


def thirds(matrix):
    return jnp.stack(split3(jnp.asarray(matrix)))


def dot(a, b):
    return jnp.dot(a, b, preferred_element_type=f32)


def dot_nt(a, b):
    return lax.dot_general(a, b, (((1,), (1,)), ((), ())), preferred_element_type=f32)


def split2(x):
    high = x.astype(bf16)
    low = (x - high.astype(f32)).astype(bf16)
    return high, low


def split3(x):
    high = x.astype(bf16)
    rest = x - high.astype(f32)
    mid = rest.astype(bf16)
    low = (rest - mid.astype(f32)).astype(bf16)
    return high, mid, low


def parts3(x):
    high, mid, low = split3(x)
    return high.astype(f32), mid.astype(f32), low.astype(f32)


def moved_exactly(rows, hot, product):
    count = rows.shape[0]
    high, mid, low = split3(rows)
    out = product(jnp.concatenate([high, mid, low], axis=0), hot)
    return out[:count] + out[count : 2 * count] + out[2 * count :]


def by_thirds(matrix_ref, x):
    high, mid, low = split3(x)
    both = jnp.concatenate([high, mid], axis=1)
    out = dot(matrix_ref[0], both) + dot(matrix_ref[1], both)
    small = dot(matrix_ref[0], low) + dot(matrix_ref[2], high)
    return out[:, : x.shape[1]] + (out[:, x.shape[1] :] + small)


def rolled(x, shift):
    return pltpu.roll(x, shift, 1)


def bonds(planes, used_oxygen):
    one = [rolled(x, SLOTS - MOLS) for x in planes]
    two = [rolled(x, SLOTS - 2 * MOLS) for x in planes]
    d1 = [x - a for x, a in zip(planes, one)]
    d2 = [x - a for x, a in zip(planes, two)]
    d3 = [a - b for a, b in zip(one, two)]
    c1 = bond_stiffness * (d1[0] * d1[0] + d1[1] * d1[1] + d1[2] * d1[2] - bond_square)
    c2 = bond_stiffness * (d2[0] * d2[0] + d2[1] * d2[1] + d2[2] * d2[2] - bond_square)
    c3 = angle_stiffness * (d3[0] * d3[0] + d3[1] * d3[1] + d3[2] * d3[2] - angle_square)
    c1, c2, c3 = c1 * used_oxygen, c2 * used_oxygen, c3 * used_oxygen
    out = []
    for k in range(3):
        a, b, c = c1 * d1[k], c2 * d2[k], c3 * d3[k]
        out.append(rolled(a - c, MOLS) + rolled(b + c, 2 * MOLS) - (a + b))
    return out


def patterns():
    lane = lax.broadcasted_iota(jnp.int32, (1, SLOTS), 1)
    is_oxygen = jnp.where(lane < MOLS, 1.0, 0.0).astype(f32)
    charge = jnp.where(lane < MOLS, charge_oxygen, charge_hydrogen).astype(f32)
    return is_oxygen, charge


def bead_rows(bead):
    row = lax.broadcasted_iota(jnp.int32, (8, SLOTS), 0)
    return (row >= 3 * bead) & (row < 3 * bead + 3), row == 6, row == 7


def left_features(xyz, norm, rows):
    _, is_norm, is_one = rows
    full = jnp.where(is_norm, norm + coulomb_soft, jnp.where(is_one, 1.0, xyz))
    h, m, l = parts3(full)
    return jnp.concatenate([h, h, m, m, h, l], axis=0).astype(bf16)


def right_features(xyz, norm, rows):
    _, is_norm, is_one = rows
    full = jnp.where(is_norm, 1.0, jnp.where(is_one, norm, -2.0 * xyz))
    h, m, l = parts3(full)
    return jnp.concatenate([h, m, h, m, l, h], axis=0).astype(bf16)


def sum_features(xyz, rows, weight):
    full = jnp.where(rows[1], 1.0, xyz) * weight
    high = full.astype(bf16).astype(f32)
    return jnp.concatenate([high, full - high], axis=0).astype(bf16)


def squared(xyz):
    return jnp.sum(xyz * xyz, axis=0, keepdims=True)


def pulled(xyz, sums, bead):
    return xyz * sums[6:7, :] - sums


def folded(out):
    return out[0:8] + out[8:16]


CHUNK = 32


class Forces:
    def __init__(self, tile_of, used_of, own_ref, next_ref, mask_ref, lj_mask_ref, near_ref, ox_ref, feats_ref, ox_feats_ref):
        self.tile_of, self.used_of, self.own_ref, self.next_ref = tile_of, used_of, own_ref, next_ref
        self.mask_ref, self.lj_mask_ref, self.near_ref, self.ox_ref = mask_ref, lj_mask_ref, near_ref, ox_ref
        self.feats_ref, self.ox_feats_ref = feats_ref, ox_feats_ref
        self.is_oxygen, self.charge = patterns()
        self.rows = [bead_rows(bead) for bead in range(2)]
        self.row = lax.broadcasted_iota(jnp.int32, (8, SLOTS), 0)
        self.lane = lax.broadcasted_iota(jnp.int32, (8, SLOTS), 1)

    def xyz(self, c, bead, cell_shift):
        shift = jnp.where(self.row == 3 * bead, 0.5 - cell_shift, 0.5)
        return jnp.where(self.rows[bead][0], self.tile_of(c) - shift, 0.0)

    def squares(self, c, bead, alone=False):
        rows, lane = self.rows[bead], self.lane
        used, used2 = self.used_of(c), self.used_of(c + 1)
        xyz, xyz2 = self.xyz(c, bead, 0.0), self.xyz(c + 1, bead, 1.0)
        norm, norm2 = squared(xyz), squared(xyz2)
        left = left_features(xyz, norm, rows).T
        right2 = right_features(xyz2, norm2, rows)
        feats = sum_features(xyz, rows, used * self.charge)
        feats2 = sum_features(xyz2, rows, used2 * self.charge)
        self.feats_ref[bead] = jnp.concatenate([feats, feats2], axis=1)
        if alone:
            self.near_ref[bead, :, SLOTS:] = dot(left, right2)
            return
        right = jnp.concatenate([right_features(xyz, norm, rows), right2], axis=1)
        self.near_ref[bead] = dot(left, right)
        used0, xyz0 = self.used_of(c - 1), self.xyz(c - 1, bead, -1.0)
        three = jnp.where(
            lane < MOLS,
            xyz0,
            jnp.where(lane < 2 * MOLS, rolled(xyz, MOLS), rolled(xyz2, 2 * MOLS)),
        )
        ox = jnp.where(
            lane[:1] < MOLS,
            used0,
            jnp.where(
                lane[:1] < 2 * MOLS,
                rolled(used, MOLS),
                jnp.where(lane[:1] < 3 * MOLS, rolled(used2, 2 * MOLS), 0.0),
            ),
        )
        right = right_features(three, squared(three) + (lennard_soft - coulomb_soft), rows)
        self.ox_ref[bead] = dot(left[:48], right)
        self.ox_feats_ref[bead] = sum_features(three, rows, ox)

    def next_sums(self, c, bead, g):
        xyz2 = self.xyz(c + 1, bead, 1.0)
        feats = self.feats_ref[bead, :, :SLOTS]
        sums = folded(dot(feats, g[0]) + dot(feats, g[1]))
        return pulled(xyz2, sums, bead) * (coulomb_scale * self.used_of(c + 1) * self.charge)

    def sums(self, c, bead):
        high, low = [], []
        for i in range(0, SLOTS, CHUNK):
            part = self.near_ref[bead, i : i + CHUNK]
            part = jnp.concatenate([part[:, :SLOTS] + self.mask_ref[i : i + CHUNK], part[:, SLOTS:]], axis=1)
            y = lax.rsqrt(part)
            h, l = split2(y * y * y)
            high.append(h)
            low.append(l)
        high, low = jnp.concatenate(high, axis=0), jnp.concatenate(low, axis=0)
        y = lax.rsqrt(self.ox_ref[bead] + self.lj_mask_ref[...])
        inverse = y * y
        cubed = (inverse * inverse) * (inverse * sigma_square**3)
        g = cubed * (cubed * (48.0 * well_depth) - 24.0 * well_depth) * inverse
        ox_high, ox_low = split2(g)
        xyz = self.xyz(c, bead, 0.0)
        used = self.used_of(c)
        feats = self.feats_ref[bead]
        near = folded(dot_nt(feats, high) + dot_nt(feats, low))
        after = self.next_sums(c, bead, (high[:, SLOTS:], low[:, SLOTS:]))
        ox_feats = self.ox_feats_ref[bead]
        ox = folded(dot_nt(ox_feats, ox_high) + dot_nt(ox_feats, ox_low))
        ox = jnp.concatenate([ox, jnp.zeros((8, SLOTS - 48), f32)], axis=1)
        force = pulled(xyz, near, bead) * (coulomb_scale * used * self.charge)
        return force + pulled(xyz, ox, bead) * (used * self.is_oxygen), after

    def first_halo(self):
        out = []
        for bead in range(2):
            self.squares(0, bead, alone=True)
        for bead in range(2):
            y = lax.rsqrt(self.near_ref[bead, :, SLOTS:])
            out.append(self.next_sums(0, bead, split2(y * y * y)))
        self.next_ref[1] = jnp.where(self.row < 3, out[0], out[1])

    def cells(self, cell_of, count):
        for bead in range(2):
            self.squares(cell_of(0), bead)

        def body(i, carry):
            c = cell_of(i)
            follows = cell_of(jnp.minimum(i + 1, count - 1))
            near0, after0 = self.sums(c, 0)
            self.squares(follows, 0)
            near1, after1 = self.sums(c, 1)
            self.squares(follows, 1)
            self.own_ref[c] = jnp.where(self.row < 3, near0, near1)
            self.next_ref[c + 1] = jnp.where(self.row < 3, after0, after1)
            return carry

        lax.fori_loop(0, count, body, 0, unroll=2)


def evolve(first_ref, second_ref, mode_in, mode_out, back_x, back_v, in_recv, out_send, out_recv, v_recv, cells, slots, group):
    b = lax.axis_index("bead")
    is_oxygen, _ = patterns()
    for kind in range(2):
        received = mode_in.at[kind, pl.ds(0, slots), :, pl.ds(0, ROWS[kind])]
        pltpu.make_async_copy(received, received, in_recv.at[kind]).wait()
    rows = [mode_in[:, slot].reshape(256, SLOTS) for slot in range(slots)]
    evolved = by_thirds(first_ref, jnp.concatenate(rows, axis=1))
    states = []
    for slot in range(slots):
        oxygens = mode_in[0, slot, 0, 6:7, :] * is_oxygen
        inverse = 1.0 - (15.0 / 16.0) * oxygens
        mine = evolved[:, SLOTS * slot : SLOTS * slot + SLOTS]
        pull = bonds([mine[32 * k : 32 * k + 32] for k in range(3)], oxygens)
        kicked = [mine[96 + 32 * k : 128 + 32 * k] + (inner_step * inverse) * pull[k] for k in range(3)]
        states.append(jnp.concatenate([mine[:96], *kicked], axis=0))
    out = by_thirds(second_ref, jnp.concatenate(states, axis=1))
    for slot in range(slots):
        mode_out[:, slot] = out[:, SLOTS * slot : SLOTS * slot + SLOTS].reshape(2, GROUP, 8, SLOTS)

    def back(kind, slot, dst, recv_sem):
        def send(i, carry):
            peer = lax.rem(b // 4 + i, 4) * 4 + i // 4
            pltpu.make_async_remote_copy(
                src_ref=mode_out.at[kind, slot, peer, pl.ds(0, 6)],
                dst_ref=dst.at[pl.ds(0, 6)],
                send_sem=out_send.at[kind],
                recv_sem=recv_sem,
                device_id=(peer, group),
                device_id_type=MESH,
            ).start()
            return carry

        lax.fori_loop(0, GROUP, send, 0)

    for slot in range(slots):
        at = cells[slot]
        back(0, slot, back_x.at[at + 1], out_recv.at[at + 1])
    for slot in range(slots):
        back(1, slot, back_v.at[cells[slot]], v_recv)


def pick(group, two):
    return jnp.where(group < SPACE // 2, two[0], two[1]) != 0


def slots_of(row):
    return [row[:q].count(row[q]) for q in range(4)]


def table(group, of, at):
    rows = [list(of(row)) for row in KEEPERS]
    out = 0
    for i in range(4):
        value = rows[0][i] if rows[0][i] == rows[1][i] else jnp.where(group < SPACE // 2, rows[0][i], rows[1][i])
        out = value if i == 0 else jnp.where(at == i, value, out)
    return out


def kernel(
    pos_hbm,
    mom_hbm,
    ids_hbm,
    first_hbm,
    second_hbm,
    out,
    pos_ref,
    mom_ref,
    ids_ref,
    first_ref,
    second_ref,
    load_sem,
    raw,
    hot,
    tiles,
    moms,
    own_ref,
    next_ref,
    mask_ref,
    lj_mask_ref,
    near_ref,
    ox_ref,
    feats_ref,
    ox_feats_ref,
    sent_v,
    mode_in,
    mode_out,
    back_x,
    back_v,
    halo_send,
    halo_recv,
    in_send,
    in_recv,
    out_send,
    out_recv,
    v_recv,
):
    b = lax.axis_index("bead")
    s = lax.axis_index("space")
    far = lax.rem(s + FLIP, SPACE)
    right = lax.rem(s + 1, SPACE)
    left = lax.rem(s + SPACE - 1, SPACE)
    x_own, z_own = b // 4, lax.rem(b, 4)
    late = (z_own >= 2) | ((z_own == 1) & pick(s, GREET_MID))

    from_cell = jnp.where(z_own == 0, 8, 0)

    def keeper(j):
        return lax.rem(j, 4) * 4 + table(s, lambda row: row, j // 4)

    def slot_of(j):
        return table(s, slots_of, j // 4)

    kept = table(far, lambda row: [row.count(z) for z in range(4)], z_own)
    kept_cells = [
        x_own + 4 * table(far, lambda row: [([q for q in range(4) if row[q] == z] + [0, 0])[k] for z in range(4)], z_own)
        for k in range(2)
    ]
    senders = table(s, lambda row: [4 * len(set(row))] * 4, 0)

    loads = [
        pltpu.make_async_copy(src, dst, load_sem.at[i])
        for i, (src, dst) in enumerate(
            ((pos_hbm, pos_ref), (mom_hbm, mom_ref), (ids_hbm, ids_ref), (first_hbm, first_ref), (second_hbm, second_ref))
        )
    ]
    for load in loads:
        load.start()

    barrier = pltpu.get_barrier_semaphore()

    def hello(peer, carry):
        pl.semaphore_signal(barrier, inc=1, device_id=(peer, far), device_id_type=MESH)
        return carry

    mode_in[...] = jnp.zeros_like(mode_in)

    @pl.when(kept > 0)
    def _():
        lax.fori_loop(0, GROUP, hello, 0)

    for who in (left, right):
        pl.semaphore_signal(barrier, inc=1, device_id=(b, who), device_id_type=MESH)

    for load in loads[:3]:
        load.wait()

    raw[...] = jnp.zeros_like(raw)
    for bead in range(2):
        for k in range(3):
            raw[pl.ds(3 * bead + k, CELLS, stride=16), :] = pos_ref[bead, k]
            raw[pl.ds(8 + 3 * bead + k, CELLS, stride=16), :] = mom_ref[bead, k]

    sub = lax.broadcasted_iota(jnp.int32, (SLOTS, SLOTS), 0)
    lane = lax.broadcasted_iota(jnp.int32, (SLOTS, SLOTS), 1)
    same = (sub % MOLS == lane % MOLS) & (sub < 3 * MOLS) & (lane < 3 * MOLS)
    mask_ref[...] = jnp.where(same, BIG, 0.0).astype(f32)
    lj_mask_ref[...] = jnp.where(lane[:48] == sub[:48] + MOLS, BIG, 0.0).astype(f32)

    ids = jnp.full((CELLS, SLOTS), SLOTS, jnp.int32)
    lane16 = lane[:CELLS]
    for t in range(3):
        padded = jnp.concatenate([ids_ref[t], jnp.zeros((CELLS, SLOTS - MOLS), jnp.int32)], axis=1)
        here = (lane16 >= t * MOLS) & (lane16 < (t + 1) * MOLS)
        ids = jnp.where(here, padded if t == 0 else rolled(padded, t * MOLS), ids)
    used_all = jnp.where(ids < SLOTS, 1.0, 0.0).astype(f32)
    above = jnp.where(sub < lane, 1.0, 0.0).astype(bf16)
    spare = dot((1.0 - used_all).astype(bf16), above)
    keys = jnp.where(ids < SLOTS, ids.astype(f32), spare + 1000.0)
    ones = jnp.ones((SLOTS, SLOTS), bf16)
    sub_f = sub.astype(f32)
    row16 = lax.broadcasted_iota(jnp.int32, (16, SLOTS), 0)

    def taken_below(c):
        key = keys[c : c + 1]
        return dot(jnp.where(key < sub_f, 1.0, jnp.where(key == sub_f, 0.5, 0.0)).astype(bf16), ones)

    ahead = [taken_below(c) for c in range(2)]
    for c in range(CELLS):
        if c + 2 < CELLS:
            ahead.append(taken_below(c + 2))
        key = keys[c : c + 1]
        spare_key = (sub_f + 1000.0) - ahead[c]
        place = jnp.where((sub_f == key) | (spare_key == key), 1.0, 0.0).astype(bf16)
        hot[c] = place
        rows = moved_exactly(raw[16 * c : 16 * c + 16], place, dot)
        rows = jnp.where(row16 == 6, used_all[c : c + 1], rows)
        tiles[c + 1] = rows[:8]
        moms[c] = rows[8:]

    def beside(ref, rows, at):
        return [
            pltpu.make_async_remote_copy(
                src_ref=ref.at[1, pl.ds(0, rows)],
                dst_ref=ref.at[CELLS + 1, pl.ds(0, rows)],
                send_sem=halo_send.at[at],
                recv_sem=halo_recv.at[at],
                device_id=(b, left),
                device_id_type=MESH,
            ),
            pltpu.make_async_remote_copy(
                src_ref=ref.at[CELLS, pl.ds(0, rows)],
                dst_ref=ref.at[0, pl.ds(0, rows)],
                send_sem=halo_send.at[at + 1],
                recv_sem=halo_recv.at[at + 1],
                device_id=(b, right),
                device_id_type=MESH,
            ),
        ]

    def send_in(kind, ref, first, cell_of, count):
        def send(i, carry):
            j = cell_of(i)
            pltpu.make_async_remote_copy(
                src_ref=ref.at[j + first, pl.ds(0, ROWS[kind])],
                dst_ref=mode_in.at[kind, slot_of(j), b, pl.ds(0, ROWS[kind])],
                send_sem=in_send.at[kind],
                recv_sem=in_recv.at[kind],
                device_id=(keeper(j), far),
                device_id_type=MESH,
            ).start()
            return carry

        lax.fori_loop(0, count, send, 0)

    def send_x():
        send_in(0, tiles, 1, lambda i: lax.rem(from_cell + i, CELLS), CELLS)

    halos = beside(tiles, 7, 0)

    def greet():
        pl.semaphore_wait(barrier, senders + 2)
        for copy in halos:
            copy.start()

    is_oxygen, _ = patterns()
    used_planes = jnp.concatenate([used_all, used_all], axis=0)
    used_ox = used_planes * is_oxygen
    inverse_mass = 1.0 - (15.0 / 16.0) * used_ox
    mass = 1.0 + 15.0 * used_ox

    def used_of(c):
        return tiles[c, 6:7, :]

    tiles_rows = tiles.reshape((CELLS + 2) * 8, SLOTS)
    moms_rows = moms.reshape(CELLS * 8, SLOTS)
    own_rows = own_ref.reshape((CELLS + 2) * 8, SLOTS)
    next_rows = next_ref.reshape((CELLS + 2) * 8, SLOTS)
    sent_rows = sent_v.reshape(CELLS * 8, SLOTS)
    back_x_rows = back_x.reshape((CELLS + 2) * 8, SLOTS)
    back_v_rows = back_v.reshape(CELLS * 8, SLOTS)

    def plane(ref, start, k):
        return jnp.concatenate(
            [ref[pl.ds(start + 3 * bead + k, CELLS, stride=8), :] for bead in range(2)], axis=0
        )

    own_ref[...] = jnp.zeros_like(own_ref)
    next_ref[...] = jnp.zeros_like(next_ref)
    scratch = (own_ref, next_ref, mask_ref, lj_mask_ref, near_ref, ox_ref, feats_ref, ox_feats_ref)
    now = Forces(lambda c: tiles[c], used_of, *scratch)
    now.cells(lambda i: i + 2, 4)
    @pl.when(late)
    def _():
        greet()
        send_x()

    now.cells(lambda i: i + 6, CELLS - 6)
    pl.when(jnp.logical_not(late))(greet)

    @pl.when(jnp.logical_not(late))
    def _():
        send_x()

    inner = bonds([plane(tiles_rows, 8, k) for k in range(3)], used_ox)

    def kicked():
        out = []
        for k in range(3):
            p = plane(moms_rows, 0, k) + (0.5 * outer_step) * (plane(own_rows, 8, k) + plane(next_rows, 8, k))
            out.append((p + (0.5 * inner_step) * inner[k]) * inverse_mass)
        return out

    for k, v in enumerate(kicked()):
        for bead in range(2):
            sent_rows[pl.ds(3 * bead + k, CELLS, stride=8), :] = v[CELLS * bead : CELLS * bead + CELLS]
    send_in(1, sent_v, 0, lambda i: 2 + lax.rem(jnp.maximum(from_cell - 2, 0) + i, CELLS - 3), CELLS - 3)
    for copy in halos:
        copy.wait()
    now.cells(lambda i: CELLS - (CELLS - 1) * i, 2)
    now.first_halo()
    for k, v in enumerate(kicked()):
        for bead in range(2):
            for c in (0, 1, CELLS - 1):
                sent_v[c, 3 * bead + k : 3 * bead + k + 1, :] = v[CELLS * bead + c : CELLS * bead + c + 1]
    send_in(1, sent_v, 0, lambda i: jnp.where(i == 2, CELLS - 1, i), 3)

    evolution = (first_ref, second_ref, mode_in, mode_out, back_x, back_v, in_recv, out_send, out_recv, v_recv)

    for load in loads[3:]:
        load.wait()

    for count in range(1, 3):

        @pl.when(kept == count)
        def _():
            evolve(*evolution, kept_cells, count, far)

    def arrived(c):
        tile = back_x.at[c, pl.ds(0, 6)]
        pltpu.make_async_copy(tile, tile, out_recv.at[c]).wait()

    halos = beside(back_x, 6, 2)
    arrived(1)
    halos[0].start()
    for c in range(2, 9):
        arrived(c)
    then = Forces(lambda c: back_x[c], used_of, *scratch)
    then.cells(lambda i: i + 2, 6)
    for c in range(CELLS, 8, -1):
        arrived(c)
        if c == CELLS:
            halos[1].start()
    then.cells(lambda i: i + 8, 8)
    for copy in halos:
        copy.wait()
    then.cells(lambda i: CELLS - (CELLS - 1) * i, 2)
    then.first_halo()
    inner = bonds([plane(back_x_rows, 8, k) for k in range(3)], used_ox)
    received = back_v.at[:, pl.ds(0, 6)]
    pltpu.make_async_copy(received, received, v_recv).wait()
    for k in range(3):
        outer = plane(own_rows, 8, k) + plane(next_rows, 8, k)
        p = mass * plane(back_v_rows, 0, k) + (0.5 * inner_step) * inner[k]
        p = p + (0.5 * outer_step) * outer
        x = plane(back_x_rows, 8, k)
        for bead in range(2):
            half = slice(CELLS * bead, CELLS * bead + CELLS)
            raw[pl.ds(3 * bead + k, CELLS, stride=16), :] = x[half]
            raw[pl.ds(8 + 3 * bead + k, CELLS, stride=16), :] = p[half]
    for c in range(CELLS):
        raw[16 * c : 16 * c + 16] = moved_exactly(raw[16 * c : 16 * c + 16], hot[c], dot_nt)
    for bead in range(2):
        for k in range(3):
            out[0, bead, k] = raw[pl.ds(3 * bead + k, CELLS, stride=16), :]
            out[1, bead, k] = raw[pl.ds(8 + 3 * bead + k, CELLS, stride=16), :]

    for kind in range(2):
        sent = sent_v.at[:, pl.ds(0, ROWS[kind])]
        pltpu.make_async_copy(sent, sent, in_send.at[kind]).wait()

    def all_back(slots):
        for kind in range(2):
            sent = mode_out.at[kind, pl.ds(0, slots), :, pl.ds(0, 6)]
            pltpu.make_async_copy(sent, sent, out_send.at[kind]).wait()

    for count in range(1, 3):
        pl.when(kept == count)(functools.partial(all_back, count))


def local(positions, momenta, molecules):
    ids = jnp.transpose(molecules, (2, 0, 1))
    first, second = propagators()
    vmem = pl.BlockSpec(memory_space=pltpu.VMEM)
    both = pl.pallas_call(
        kernel,
        out_shape=jax.ShapeDtypeStruct((2, *positions.shape), f32),
        in_specs=[pl.BlockSpec(memory_space=pl.ANY)] * 5,
        out_specs=vmem,
        scratch_shapes=[
            pltpu.VMEM(positions.shape, f32),
            pltpu.VMEM(momenta.shape, f32),
            pltpu.VMEM(ids.shape, jnp.int32),
            pltpu.VMEM((3, 192, 256), bf16),
            pltpu.VMEM((3, 256, 192), bf16),
            pltpu.SemaphoreType.DMA((5,)),
            pltpu.VMEM((CELLS * 16, SLOTS), f32),
            pltpu.VMEM((CELLS, SLOTS, SLOTS), bf16),
            pltpu.VMEM((CELLS + 2, 8, SLOTS), f32),
            pltpu.VMEM((CELLS, 8, SLOTS), f32),
            pltpu.VMEM((CELLS + 2, 8, SLOTS), f32),
            pltpu.VMEM((CELLS + 2, 8, SLOTS), f32),
            pltpu.VMEM((SLOTS, SLOTS), f32),
            pltpu.VMEM((48, SLOTS), f32),
            pltpu.VMEM((2, SLOTS, 2 * SLOTS), f32),
            pltpu.VMEM((2, 48, SLOTS), f32),
            pltpu.VMEM((2, 16, 2 * SLOTS), bf16),
            pltpu.VMEM((2, 16, SLOTS), bf16),
            pltpu.VMEM((CELLS, 8, SLOTS), f32),
            pltpu.VMEM((2, 2, GROUP, 8, SLOTS), f32),
            pltpu.VMEM((2, 2, GROUP, 8, SLOTS), f32),
            pltpu.VMEM((CELLS + 2, 8, SLOTS), f32),
            pltpu.VMEM((CELLS, 8, SLOTS), f32),
            pltpu.SemaphoreType.DMA((4,)),
            pltpu.SemaphoreType.DMA((4,)),
            pltpu.SemaphoreType.DMA((2,)),
            pltpu.SemaphoreType.DMA((2,)),
            pltpu.SemaphoreType.DMA((2,)),
            pltpu.SemaphoreType.DMA((CELLS + 2,)),
            pltpu.SemaphoreType.DMA,
        ],
        compiler_params=pltpu.CompilerParams(collective_id=0, has_side_effects=True),
    )(positions, momenta, ids, thirds(first), thirds(second))
    return both[0], both[1]


def solution(mesh):
    wide = P("bead", None, "space", None)
    return jax.shard_map(
        local,
        mesh=mesh,
        in_specs=(wide, wide, P("space", None, None)),
        out_specs=(wide, wide),
        check_vma=False,
    )
```

```python
import functools

import jax
import jax.numpy as jnp
import numpy as np
from jax import lax
from jax.experimental import pallas as pl
from jax.experimental.pallas import tpu as pltpu
from jax.sharding import PartitionSpec as P

MESH = pl.DeviceIdType.MESH

SLOTS = 128
MOLS = 42
CELLS = 16
BEADS = 32
GROUP = 16
SPACE = 32
KEEPERS = ((0, 3, 1, 2), (0, 1, 1, 3))
GREET_MID = (0, 1)
ROWS = (7, 6)
FLIP = 16

charge_oxygen = -0.8476
charge_hydrogen = 0.4238
coulomb_scale = 24.0
coulomb_soft = 0.004
well_depth = 0.02
sigma_square = 0.0841
lennard_soft = 0.04
bond_stiffness = 20000.0
bond_square = 0.0081
angle_stiffness = 5000.0
angle_square = 0.0204
cycle_frequency = 60.0
outer_step = 0.02
inner_step = 0.01
BIG = 2.0**100

f32 = jnp.float32
bf16 = jnp.bfloat16


def propagators():
    ids = np.arange(BEADS)
    angles = 2.0 * np.pi / BEADS * (ids[:, None] * ids[None, :] % BEADS)
    half = BEADS // 2
    col = ids[None, :]
    transform = np.where(
        col == 0,
        np.sqrt(1.0 / BEADS),
        np.where(
            col < half,
            np.sqrt(2.0 / BEADS) * np.cos(angles),
            np.where(
                col == half,
                np.sqrt(1.0 / BEADS) * np.cos(angles),
                np.sqrt(2.0 / BEADS) * np.sin(angles),
            ),
        ),
    )
    freq = 2.0 * cycle_frequency * np.sin(np.pi * ids / BEADS)
    cosk = np.cos(freq * inner_step)
    springk = freq * np.sin(freq * inner_step)
    driftk = np.where(ids == 0, inner_step, np.sin(freq * inner_step) / np.where(ids == 0, 1.0, freq))
    on = [transform @ np.diag(v) @ transform.T for v in (cosk, driftk, -springk)]
    step = [[on[0], on[1]], [on[2], on[0]]]
    tile = np.zeros((2, 3, BEADS), int)
    plane = np.zeros((2, 3, BEADS), int)
    for kind in range(2):
        for k in range(3):
            for j in range(BEADS):
                tile[kind, k, j] = 128 * kind + 8 * (j // 2) + 3 * (j % 2) + k
                plane[kind, k, j] = 96 * kind + 32 * k + j
    first = np.zeros((192, 256))
    second = np.zeros((256, 192))
    for a in range(2):
        for b in range(2):
            for k in range(3):
                first[np.ix_(plane[a, k], tile[b, k])] = step[a][b]
                second[np.ix_(tile[a, k], plane[b, k])] = step[a][b]
    return first.astype(np.float32), second.astype(np.float32)


def thirds(matrix):
    return jnp.stack(split3(jnp.asarray(matrix)))


def dot(a, b):
    return jnp.dot(a, b, preferred_element_type=f32)


def dot_nt(a, b):
    return lax.dot_general(a, b, (((1,), (1,)), ((), ())), preferred_element_type=f32)


def split2(x):
    high = x.astype(bf16)
    low = (x - high.astype(f32)).astype(bf16)
    return high, low


def split3(x):
    high = x.astype(bf16)
    rest = x - high.astype(f32)
    mid = rest.astype(bf16)
    low = (rest - mid.astype(f32)).astype(bf16)
    return high, mid, low


def parts3(x):
    high, mid, low = split3(x)
    return high.astype(f32), mid.astype(f32), low.astype(f32)


def moved_exactly(rows, hot, product):
    count = rows.shape[0]
    high, mid, low = split3(rows)
    out = product(jnp.concatenate([high, mid, low], axis=0), hot)
    return out[:count] + out[count : 2 * count] + out[2 * count :]


def by_thirds(matrix_ref, x):
    high, mid, low = split3(x)
    both = jnp.concatenate([high, mid], axis=1)
    out = dot(matrix_ref[0], both) + dot(matrix_ref[1], both)
    small = dot(matrix_ref[0], low) + dot(matrix_ref[2], high)
    return out[:, : x.shape[1]] + (out[:, x.shape[1] :] + small)


def rolled(x, shift):
    return pltpu.roll(x, shift, 1)


def bonds(planes, used_oxygen):
    one = [rolled(x, SLOTS - MOLS) for x in planes]
    two = [rolled(x, SLOTS - 2 * MOLS) for x in planes]
    d1 = [x - a for x, a in zip(planes, one)]
    d2 = [x - a for x, a in zip(planes, two)]
    d3 = [a - b for a, b in zip(one, two)]
    c1 = bond_stiffness * (d1[0] * d1[0] + d1[1] * d1[1] + d1[2] * d1[2] - bond_square)
    c2 = bond_stiffness * (d2[0] * d2[0] + d2[1] * d2[1] + d2[2] * d2[2] - bond_square)
    c3 = angle_stiffness * (d3[0] * d3[0] + d3[1] * d3[1] + d3[2] * d3[2] - angle_square)
    c1, c2, c3 = c1 * used_oxygen, c2 * used_oxygen, c3 * used_oxygen
    out = []
    for k in range(3):
        a, b, c = c1 * d1[k], c2 * d2[k], c3 * d3[k]
        out.append(rolled(a - c, MOLS) + rolled(b + c, 2 * MOLS) - (a + b))
    return out


def patterns():
    lane = lax.broadcasted_iota(jnp.int32, (1, SLOTS), 1)
    is_oxygen = jnp.where(lane < MOLS, 1.0, 0.0).astype(f32)
    charge = jnp.where(lane < MOLS, charge_oxygen, charge_hydrogen).astype(f32)
    return is_oxygen, charge


def bead_rows(bead):
    row = lax.broadcasted_iota(jnp.int32, (8, SLOTS), 0)
    return (row >= 3 * bead) & (row < 3 * bead + 3), row == 6, row == 7


def left_features(xyz, norm, rows):
    _, is_norm, is_one = rows
    full = jnp.where(is_norm, norm + coulomb_soft, jnp.where(is_one, 1.0, xyz))
    h, m, l = parts3(full)
    return jnp.concatenate([h, h, m, m, h, l], axis=0).astype(bf16)


def right_features(xyz, norm, rows):
    _, is_norm, is_one = rows
    full = jnp.where(is_norm, 1.0, jnp.where(is_one, norm, -2.0 * xyz))
    h, m, l = parts3(full)
    return jnp.concatenate([h, m, h, m, l, h], axis=0).astype(bf16)


def sum_features(xyz, rows, weight):
    full = jnp.where(rows[1], 1.0, xyz) * weight
    high = full.astype(bf16).astype(f32)
    return jnp.concatenate([high, full - high], axis=0).astype(bf16)


def squared(xyz):
    return jnp.sum(xyz * xyz, axis=0, keepdims=True)


def pulled(xyz, sums, bead):
    return xyz * sums[6:7, :] - sums


def folded(out):
    return out[0:8] + out[8:16]


CHUNK = 32


class Forces:
    def __init__(self, tile_of, used_of, own_ref, next_ref, mask_ref, lj_mask_ref, near_ref, ox_ref, feats_ref, ox_feats_ref):
        self.tile_of, self.used_of, self.own_ref, self.next_ref = tile_of, used_of, own_ref, next_ref
        self.mask_ref, self.lj_mask_ref, self.near_ref, self.ox_ref = mask_ref, lj_mask_ref, near_ref, ox_ref
        self.feats_ref, self.ox_feats_ref = feats_ref, ox_feats_ref
        self.is_oxygen, self.charge = patterns()
        self.rows = [bead_rows(bead) for bead in range(2)]
        self.row = lax.broadcasted_iota(jnp.int32, (8, SLOTS), 0)
        self.lane = lax.broadcasted_iota(jnp.int32, (8, SLOTS), 1)

    def xyz(self, c, bead, cell_shift):
        shift = jnp.where(self.row == 3 * bead, 0.5 - cell_shift, 0.5)
        return jnp.where(self.rows[bead][0], self.tile_of(c) - shift, 0.0)

    def squares(self, c, bead, alone=False):
        rows, lane = self.rows[bead], self.lane
        used, used2 = self.used_of(c), self.used_of(c + 1)
        xyz, xyz2 = self.xyz(c, bead, 0.0), self.xyz(c + 1, bead, 1.0)
        norm, norm2 = squared(xyz), squared(xyz2)
        left = left_features(xyz, norm, rows).T
        right2 = right_features(xyz2, norm2, rows)
        feats = sum_features(xyz, rows, used * self.charge)
        feats2 = sum_features(xyz2, rows, used2 * self.charge)
        self.feats_ref[bead] = jnp.concatenate([feats, feats2], axis=1)
        if alone:
            self.near_ref[bead, :, SLOTS:] = dot(left, right2)
            return
        right = jnp.concatenate([right_features(xyz, norm, rows), right2], axis=1)
        self.near_ref[bead] = dot(left, right)
        used0, xyz0 = self.used_of(c - 1), self.xyz(c - 1, bead, -1.0)
        three = jnp.where(
            lane < MOLS,
            xyz0,
            jnp.where(lane < 2 * MOLS, rolled(xyz, MOLS), rolled(xyz2, 2 * MOLS)),
        )
        ox = jnp.where(
            lane[:1] < MOLS,
            used0,
            jnp.where(
                lane[:1] < 2 * MOLS,
                rolled(used, MOLS),
                jnp.where(lane[:1] < 3 * MOLS, rolled(used2, 2 * MOLS), 0.0),
            ),
        )
        right = right_features(three, squared(three) + (lennard_soft - coulomb_soft), rows)
        self.ox_ref[bead] = dot(left[:48], right)
        self.ox_feats_ref[bead] = sum_features(three, rows, ox)

    def next_sums(self, c, bead, g):
        xyz2 = self.xyz(c + 1, bead, 1.0)
        feats = self.feats_ref[bead, :, :SLOTS]
        sums = folded(dot(feats, g[0]) + dot(feats, g[1]))
        return pulled(xyz2, sums, bead) * (coulomb_scale * self.used_of(c + 1) * self.charge)

    def sums(self, c, bead):
        high, low = [], []
        for i in range(0, SLOTS, CHUNK):
            part = self.near_ref[bead, i : i + CHUNK]
            part = jnp.concatenate([part[:, :SLOTS] + self.mask_ref[i : i + CHUNK], part[:, SLOTS:]], axis=1)
            y = lax.rsqrt(part)
            h, l = split2(y * y * y)
            high.append(h)
            low.append(l)
        high, low = jnp.concatenate(high, axis=0), jnp.concatenate(low, axis=0)
        y = lax.rsqrt(self.ox_ref[bead] + self.lj_mask_ref[...])
        inverse = y * y
        cubed = (inverse * inverse) * (inverse * sigma_square**3)
        g = cubed * (cubed * (48.0 * well_depth) - 24.0 * well_depth) * inverse
        ox_high, ox_low = split2(g)
        xyz = self.xyz(c, bead, 0.0)
        used = self.used_of(c)
        feats = self.feats_ref[bead]
        near = folded(dot_nt(feats, high) + dot_nt(feats, low))
        after = self.next_sums(c, bead, (high[:, SLOTS:], low[:, SLOTS:]))
        ox_feats = self.ox_feats_ref[bead]
        ox = folded(dot_nt(ox_feats, ox_high) + dot_nt(ox_feats, ox_low))
        ox = jnp.concatenate([ox, jnp.zeros((8, SLOTS - 48), f32)], axis=1)
        force = pulled(xyz, near, bead) * (coulomb_scale * used * self.charge)
        return force + pulled(xyz, ox, bead) * (used * self.is_oxygen), after

    def first_halo(self):
        out = []
        for bead in range(2):
            self.squares(0, bead, alone=True)
        for bead in range(2):
            y = lax.rsqrt(self.near_ref[bead, :, SLOTS:])
            out.append(self.next_sums(0, bead, split2(y * y * y)))
        self.next_ref[1] = jnp.where(self.row < 3, out[0], out[1])

    def cells(self, cell_of, count):
        for bead in range(2):
            self.squares(cell_of(0), bead)

        def body(i, carry):
            c = cell_of(i)
            follows = cell_of(jnp.minimum(i + 1, count - 1))
            near0, after0 = self.sums(c, 0)
            self.squares(follows, 0)
            near1, after1 = self.sums(c, 1)
            self.squares(follows, 1)
            self.own_ref[c] = jnp.where(self.row < 3, near0, near1)
            self.next_ref[c + 1] = jnp.where(self.row < 3, after0, after1)
            return carry

        lax.fori_loop(0, count, body, 0, unroll=2)


def evolve(first_ref, second_ref, mode_in, mode_out, back_x, back_v, in_recv, out_send, out_recv, v_recv, cells, slots, group):
    b = lax.axis_index("bead")
    is_oxygen, _ = patterns()
    for kind in range(2):
        received = mode_in.at[kind, pl.ds(0, slots), :, pl.ds(0, ROWS[kind])]
        pltpu.make_async_copy(received, received, in_recv.at[kind]).wait()
    rows = [mode_in[:, slot].reshape(256, SLOTS) for slot in range(slots)]
    evolved = by_thirds(first_ref, jnp.concatenate(rows, axis=1))
    states = []
    for slot in range(slots):
        oxygens = mode_in[0, slot, 0, 6:7, :] * is_oxygen
        inverse = 1.0 - (15.0 / 16.0) * oxygens
        mine = evolved[:, SLOTS * slot : SLOTS * slot + SLOTS]
        pull = bonds([mine[32 * k : 32 * k + 32] for k in range(3)], oxygens)
        kicked = [mine[96 + 32 * k : 128 + 32 * k] + (inner_step * inverse) * pull[k] for k in range(3)]
        states.append(jnp.concatenate([mine[:96], *kicked], axis=0))
    def back(kind, slot, dst, recv_sem):
        def send(i, carry):
            peer = lax.rem(b // 4 + i, 4) * 4 + i // 4
            pltpu.make_async_remote_copy(
                src_ref=mode_out.at[kind, slot, peer, pl.ds(0, 6)],
                dst_ref=dst.at[pl.ds(0, 6)],
                send_sem=out_send.at[kind],
                recv_sem=recv_sem,
                device_id=(peer, group),
                device_id_type=MESH,
            ).start()
            return carry

        lax.fori_loop(0, GROUP, send, 0)

    state = jnp.concatenate(states, axis=1)
    for kind in range(2):
        out = by_thirds(second_ref.at[:, pl.ds(128 * kind, 128)], state)
        for slot in range(slots):
            mode_out[kind, slot] = out[:, SLOTS * slot : SLOTS * slot + SLOTS].reshape(GROUP, 8, SLOTS)
        for slot in range(slots):
            at = cells[slot]
            if kind == 0:
                back(0, slot, back_x.at[at + 1], out_recv.at[at + 1])
            else:
                back(1, slot, back_v.at[at], v_recv)


def pick(group, two):
    return jnp.where(group < SPACE // 2, two[0], two[1]) != 0


def slots_of(row):
    return [row[:q].count(row[q]) for q in range(4)]


def table(group, of, at):
    rows = [list(of(row)) for row in KEEPERS]
    out = 0
    for i in range(4):
        value = rows[0][i] if rows[0][i] == rows[1][i] else jnp.where(group < SPACE // 2, rows[0][i], rows[1][i])
        out = value if i == 0 else jnp.where(at == i, value, out)
    return out


def kernel(
    pos_hbm,
    mom_hbm,
    ids_hbm,
    first_hbm,
    second_hbm,
    out,
    pos_ref,
    mom_ref,
    ids_ref,
    first_ref,
    second_ref,
    load_sem,
    raw,
    hot,
    tiles,
    moms,
    own_ref,
    next_ref,
    mask_ref,
    lj_mask_ref,
    near_ref,
    ox_ref,
    feats_ref,
    ox_feats_ref,
    sent_v,
    mode_in,
    mode_out,
    back_x,
    back_v,
    halo_send,
    halo_recv,
    in_send,
    in_recv,
    out_send,
    out_recv,
    v_recv,
):
    b = lax.axis_index("bead")
    s = lax.axis_index("space")
    far = lax.rem(s + FLIP, SPACE)
    right = lax.rem(s + 1, SPACE)
    left = lax.rem(s + SPACE - 1, SPACE)
    x_own, z_own = b // 4, lax.rem(b, 4)
    late = (z_own >= 2) | ((z_own == 1) & pick(s, GREET_MID))

    from_cell = jnp.where(z_own == 0, 8, 0)

    def keeper(j):
        return lax.rem(j, 4) * 4 + table(s, lambda row: row, j // 4)

    def slot_of(j):
        return table(s, slots_of, j // 4)

    kept = table(far, lambda row: [row.count(z) for z in range(4)], z_own)
    kept_cells = [
        x_own + 4 * table(far, lambda row: [([q for q in range(4) if row[q] == z] + [0, 0])[k] for z in range(4)], z_own)
        for k in range(2)
    ]
    senders = table(s, lambda row: [4 * len(set(row))] * 4, 0)

    loads = [
        pltpu.make_async_copy(src, dst, load_sem.at[i])
        for i, (src, dst) in enumerate(
            ((pos_hbm, pos_ref), (mom_hbm, mom_ref), (ids_hbm, ids_ref), (first_hbm, first_ref), (second_hbm, second_ref))
        )
    ]
    for load in loads:
        load.start()

    barrier = pltpu.get_barrier_semaphore()

    def hello(peer, carry):
        pl.semaphore_signal(barrier, inc=1, device_id=(peer, far), device_id_type=MESH)
        return carry

    mode_in[...] = jnp.zeros_like(mode_in)

    @pl.when(kept > 0)
    def _():
        lax.fori_loop(0, GROUP, hello, 0)

    for who in (left, right):
        pl.semaphore_signal(barrier, inc=1, device_id=(b, who), device_id_type=MESH)

    for load in loads[:3]:
        load.wait()

    raw[...] = jnp.zeros_like(raw)
    for bead in range(2):
        for k in range(3):
            raw[pl.ds(3 * bead + k, CELLS, stride=16), :] = pos_ref[bead, k]
            raw[pl.ds(8 + 3 * bead + k, CELLS, stride=16), :] = mom_ref[bead, k]

    sub = lax.broadcasted_iota(jnp.int32, (SLOTS, SLOTS), 0)
    lane = lax.broadcasted_iota(jnp.int32, (SLOTS, SLOTS), 1)
    same = (sub % MOLS == lane % MOLS) & (sub < 3 * MOLS) & (lane < 3 * MOLS)
    mask_ref[...] = jnp.where(same, BIG, 0.0).astype(f32)
    lj_mask_ref[...] = jnp.where(lane[:48] == sub[:48] + MOLS, BIG, 0.0).astype(f32)

    ids = jnp.full((CELLS, SLOTS), SLOTS, jnp.int32)
    lane16 = lane[:CELLS]
    for t in range(3):
        padded = jnp.concatenate([ids_ref[t], jnp.zeros((CELLS, SLOTS - MOLS), jnp.int32)], axis=1)
        here = (lane16 >= t * MOLS) & (lane16 < (t + 1) * MOLS)
        ids = jnp.where(here, padded if t == 0 else rolled(padded, t * MOLS), ids)
    used_all = jnp.where(ids < SLOTS, 1.0, 0.0).astype(f32)
    above = jnp.where(sub < lane, 1.0, 0.0).astype(bf16)
    spare = dot((1.0 - used_all).astype(bf16), above)
    keys = jnp.where(ids < SLOTS, ids.astype(f32), spare + 1000.0)
    ones = jnp.ones((SLOTS, SLOTS), bf16)
    sub_f = sub.astype(f32)
    row16 = lax.broadcasted_iota(jnp.int32, (16, SLOTS), 0)

    def taken_below(c):
        key = keys[c : c + 1]
        return dot(jnp.where(key < sub_f, 1.0, jnp.where(key == sub_f, 0.5, 0.0)).astype(bf16), ones)

    ahead = [taken_below(c) for c in range(2)]
    for c in range(CELLS):
        if c + 2 < CELLS:
            ahead.append(taken_below(c + 2))
        key = keys[c : c + 1]
        spare_key = (sub_f + 1000.0) - ahead[c]
        place = jnp.where((sub_f == key) | (spare_key == key), 1.0, 0.0).astype(bf16)
        hot[c] = place
        rows = moved_exactly(raw[16 * c : 16 * c + 16], place, dot)
        rows = jnp.where(row16 == 6, used_all[c : c + 1], rows)
        tiles[c + 1] = rows[:8]
        moms[c] = rows[8:]

    def beside(ref, rows, at):
        return [
            pltpu.make_async_remote_copy(
                src_ref=ref.at[1, pl.ds(0, rows)],
                dst_ref=ref.at[CELLS + 1, pl.ds(0, rows)],
                send_sem=halo_send.at[at],
                recv_sem=halo_recv.at[at],
                device_id=(b, left),
                device_id_type=MESH,
            ),
            pltpu.make_async_remote_copy(
                src_ref=ref.at[CELLS, pl.ds(0, rows)],
                dst_ref=ref.at[0, pl.ds(0, rows)],
                send_sem=halo_send.at[at + 1],
                recv_sem=halo_recv.at[at + 1],
                device_id=(b, right),
                device_id_type=MESH,
            ),
        ]

    def send_in(kind, ref, first, cell_of, count):
        def send(i, carry):
            j = cell_of(i)
            pltpu.make_async_remote_copy(
                src_ref=ref.at[j + first, pl.ds(0, ROWS[kind])],
                dst_ref=mode_in.at[kind, slot_of(j), b, pl.ds(0, ROWS[kind])],
                send_sem=in_send.at[kind],
                recv_sem=in_recv.at[kind],
                device_id=(keeper(j), far),
                device_id_type=MESH,
            ).start()
            return carry

        lax.fori_loop(0, count, send, 0)

    def send_x():
        send_in(0, tiles, 1, lambda i: lax.rem(from_cell + i, CELLS), CELLS)

    halos = beside(tiles, 7, 0)

    def greet():
        pl.semaphore_wait(barrier, senders + 2)
        for copy in halos:
            copy.start()

    is_oxygen, _ = patterns()
    used_planes = jnp.concatenate([used_all, used_all], axis=0)
    used_ox = used_planes * is_oxygen
    inverse_mass = 1.0 - (15.0 / 16.0) * used_ox
    mass = 1.0 + 15.0 * used_ox

    def used_of(c):
        return tiles[c, 6:7, :]

    tiles_rows = tiles.reshape((CELLS + 2) * 8, SLOTS)
    moms_rows = moms.reshape(CELLS * 8, SLOTS)
    own_rows = own_ref.reshape((CELLS + 2) * 8, SLOTS)
    next_rows = next_ref.reshape((CELLS + 2) * 8, SLOTS)
    sent_rows = sent_v.reshape(CELLS * 8, SLOTS)
    back_x_rows = back_x.reshape((CELLS + 2) * 8, SLOTS)
    back_v_rows = back_v.reshape(CELLS * 8, SLOTS)

    def plane(ref, start, k):
        return jnp.concatenate(
            [ref[pl.ds(start + 3 * bead + k, CELLS, stride=8), :] for bead in range(2)], axis=0
        )

    own_ref[...] = jnp.zeros_like(own_ref)
    next_ref[...] = jnp.zeros_like(next_ref)
    scratch = (own_ref, next_ref, mask_ref, lj_mask_ref, near_ref, ox_ref, feats_ref, ox_feats_ref)
    now = Forces(lambda c: tiles[c], used_of, *scratch)
    now.cells(lambda i: i + 2, 4)
    @pl.when(late)
    def _():
        greet()
        send_x()

    now.cells(lambda i: i + 6, CELLS - 6)
    pl.when(jnp.logical_not(late))(greet)

    @pl.when(jnp.logical_not(late))
    def _():
        send_x()

    inner = bonds([plane(tiles_rows, 8, k) for k in range(3)], used_ox)

    def kicked():
        out = []
        for k in range(3):
            p = plane(moms_rows, 0, k) + (0.5 * outer_step) * (plane(own_rows, 8, k) + plane(next_rows, 8, k))
            out.append((p + (0.5 * inner_step) * inner[k]) * inverse_mass)
        return out

    for k, v in enumerate(kicked()):
        for bead in range(2):
            sent_rows[pl.ds(3 * bead + k, CELLS, stride=8), :] = v[CELLS * bead : CELLS * bead + CELLS]
    send_in(1, sent_v, 0, lambda i: 2 + lax.rem(jnp.maximum(from_cell - 2, 0) + i, CELLS - 3), CELLS - 3)
    for copy in halos:
        copy.wait()
    now.cells(lambda i: CELLS - (CELLS - 1) * i, 2)
    now.first_halo()
    for k, v in enumerate(kicked()):
        for bead in range(2):
            for c in (0, 1, CELLS - 1):
                sent_v[c, 3 * bead + k : 3 * bead + k + 1, :] = v[CELLS * bead + c : CELLS * bead + c + 1]
    send_in(1, sent_v, 0, lambda i: jnp.where(i == 2, CELLS - 1, i), 3)

    evolution = (first_ref, second_ref, mode_in, mode_out, back_x, back_v, in_recv, out_send, out_recv, v_recv)

    for load in loads[3:]:
        load.wait()

    for count in range(1, 3):

        @pl.when(kept == count)
        def _():
            evolve(*evolution, kept_cells, count, far)

    def arrived(c):
        tile = back_x.at[c, pl.ds(0, 6)]
        pltpu.make_async_copy(tile, tile, out_recv.at[c]).wait()

    halos = beside(back_x, 6, 2)
    arrived(1)
    halos[0].start()
    for c in range(2, 9):
        arrived(c)
    then = Forces(lambda c: back_x[c], used_of, *scratch)
    then.cells(lambda i: i + 2, 6)
    for c in range(CELLS, 8, -1):
        arrived(c)
        if c == CELLS:
            halos[1].start()
    then.cells(lambda i: i + 8, 8)
    for copy in halos:
        copy.wait()
    then.cells(lambda i: CELLS - (CELLS - 1) * i, 2)
    then.first_halo()
    inner = bonds([plane(back_x_rows, 8, k) for k in range(3)], used_ox)
    received = back_v.at[:, pl.ds(0, 6)]
    pltpu.make_async_copy(received, received, v_recv).wait()
    for k in range(3):
        outer = plane(own_rows, 8, k) + plane(next_rows, 8, k)
        p = mass * plane(back_v_rows, 0, k) + (0.5 * inner_step) * inner[k]
        p = p + (0.5 * outer_step) * outer
        x = plane(back_x_rows, 8, k)
        for bead in range(2):
            half = slice(CELLS * bead, CELLS * bead + CELLS)
            raw[pl.ds(3 * bead + k, CELLS, stride=16), :] = x[half]
            raw[pl.ds(8 + 3 * bead + k, CELLS, stride=16), :] = p[half]
    for c in range(CELLS):
        raw[16 * c : 16 * c + 16] = moved_exactly(raw[16 * c : 16 * c + 16], hot[c], dot_nt)
    for bead in range(2):
        for k in range(3):
            out[0, bead, k] = raw[pl.ds(3 * bead + k, CELLS, stride=16), :]
            out[1, bead, k] = raw[pl.ds(8 + 3 * bead + k, CELLS, stride=16), :]

    for kind in range(2):
        sent = sent_v.at[:, pl.ds(0, ROWS[kind])]
        pltpu.make_async_copy(sent, sent, in_send.at[kind]).wait()

    def all_back(slots):
        for kind in range(2):
            sent = mode_out.at[kind, pl.ds(0, slots), :, pl.ds(0, 6)]
            pltpu.make_async_copy(sent, sent, out_send.at[kind]).wait()

    for count in range(1, 3):
        pl.when(kept == count)(functools.partial(all_back, count))


def local(positions, momenta, molecules):
    ids = jnp.transpose(molecules, (2, 0, 1))
    first, second = propagators()
    vmem = pl.BlockSpec(memory_space=pltpu.VMEM)
    both = pl.pallas_call(
        kernel,
        out_shape=jax.ShapeDtypeStruct((2, *positions.shape), f32),
        in_specs=[pl.BlockSpec(memory_space=pl.ANY)] * 5,
        out_specs=vmem,
        scratch_shapes=[
            pltpu.VMEM(positions.shape, f32),
            pltpu.VMEM(momenta.shape, f32),
            pltpu.VMEM(ids.shape, jnp.int32),
            pltpu.VMEM((3, 192, 256), bf16),
            pltpu.VMEM((3, 256, 192), bf16),
            pltpu.SemaphoreType.DMA((5,)),
            pltpu.VMEM((CELLS * 16, SLOTS), f32),
            pltpu.VMEM((CELLS, SLOTS, SLOTS), bf16),
            pltpu.VMEM((CELLS + 2, 8, SLOTS), f32),
            pltpu.VMEM((CELLS, 8, SLOTS), f32),
            pltpu.VMEM((CELLS + 2, 8, SLOTS), f32),
            pltpu.VMEM((CELLS + 2, 8, SLOTS), f32),
            pltpu.VMEM((SLOTS, SLOTS), f32),
            pltpu.VMEM((48, SLOTS), f32),
            pltpu.VMEM((2, SLOTS, 2 * SLOTS), f32),
            pltpu.VMEM((2, 48, SLOTS), f32),
            pltpu.VMEM((2, 16, 2 * SLOTS), bf16),
            pltpu.VMEM((2, 16, SLOTS), bf16),
            pltpu.VMEM((CELLS, 8, SLOTS), f32),
            pltpu.VMEM((2, 2, GROUP, 8, SLOTS), f32),
            pltpu.VMEM((2, 2, GROUP, 8, SLOTS), f32),
            pltpu.VMEM((CELLS + 2, 8, SLOTS), f32),
            pltpu.VMEM((CELLS, 8, SLOTS), f32),
            pltpu.SemaphoreType.DMA((4,)),
            pltpu.SemaphoreType.DMA((4,)),
            pltpu.SemaphoreType.DMA((2,)),
            pltpu.SemaphoreType.DMA((2,)),
            pltpu.SemaphoreType.DMA((2,)),
            pltpu.SemaphoreType.DMA((CELLS + 2,)),
            pltpu.SemaphoreType.DMA,
        ],
        compiler_params=pltpu.CompilerParams(collective_id=0, has_side_effects=True),
    )(positions, momenta, ids, thirds(first), thirds(second))
    return both[0], both[1]


def solution(mesh):
    wide = P("bead", None, "space", None)
    return jax.shard_map(
        local,
        mesh=mesh,
        in_specs=(wide, wide, P("space", None, None)),
        out_specs=(wide, wide),
        check_vma=False,
    )
```
